32 devices in a mesh: blk: 8 (over z, y), frames: 4 (over x, core).
Axes of the slice: x: 2, y: 2, z: 4, core: 2. Of those that a mesh axis runs over, the one named last changes fastest.
Arguments:
- coarse_query: bfloat16 [64, 16, 256], P('blk'), may hold values from -125 to 125
- coarse_feat: bfloat16 [16, 8160, 256], P('frames', 'blk'), may hold values from -61 to 61
- fine_query: bfloat16 [64, 128], P(('blk', 'frames')), may hold values from -175 to 175
- fine_tiles: bfloat16 [16, 512, 64, 128], P('frames', 'blk'), may hold values from -61 to 61
- track_pos: int32 [2, 16, 64], P(None, None, ('blk', 'frames')), may hold values from 0 to 959, as said below
- tile_list: int32 [16, 8, 4, 8], P('frames', 'blk'), may hold values from 0 to 63, as said below
- tile_valid: int32 [16, 8, 4, 8], P('frames', 'blk'), may hold values from 0 to 1, as said below
Outputs:
- coarse_pos: float32 [2, 16, 64], P(None, 'frames', 'blk')
- fine_offset: float32 [2, 16, 64], P(None, None, ('blk', 'frames'))
The draws below stay inside these ranges and needn't reach their ends.
Inputs may be any that keep to these rules, and one draw needn't show every extreme that they name: `tile_list`: in each list the valid slots come first and name distinct tiles of the group's window; padded slots hold 63; in every frame and group some owner's list is full. `tile_valid`: each list has at least 4 valid slots. `track_pos`: rows lie below 544 and columns below 960.
All inputs are finite; a program needn't handle non-finite values.
Results may differ from the reference program's by a relative error of at most 0.0003.
Values may be sent and summed in bfloat16 or wider, within the bound.
No kernel may reach another device: no remote copies, remote signals or barrier semaphores. Data moves between devices by JAX's collectives and lax.ppermute only.
A program may use at most 192 MiB of HBM per device.

```python
import math
import jax
import jax.numpy as jnp
from jax import lax

C = 256
CF = 128
GH = 68
GW = 120
TILE = 8
SUP = 16
CAP = 8
TR_OWN = 2
FT = 64
OWNERS = 4
GROUPS = 8
WIN = 16
TRACKS = 64
POS = 8160
REG = 1020
CELLS = 64


def plan_lists(key):
    base_key = jax.random.fold_in(key, 101)
    keys = jax.random.split(base_key, 6)
    starts = jax.random.randint(keys[0], (WIN, GROUPS, OWNERS), 0, FT - 2 * CAP + 1)
    counts = jax.random.randint(keys[1], (WIN, GROUPS, OWNERS), max(CAP // 2, 1), CAP + 1)
    full_owner = jax.random.randint(keys[2], (WIN, GROUPS, 1), 0, OWNERS)
    counts = jnp.where(jnp.arange(OWNERS)[None, None, :] == full_owner, CAP, counts)
    ranks = jax.random.randint(keys[3], (WIN, GROUPS, OWNERS, 2 * CAP), 0, 1 << 20) * (2 * CAP) + jnp.arange(2 * CAP)
    offsets = jnp.argsort(ranks, axis=-1)[..., :CAP].astype(jnp.int32)
    valid = jnp.arange(CAP)[None, None, None, :] < counts[..., None]
    ids = jnp.where(valid, starts[..., None] + offsets, FT - 1).astype(jnp.int32)
    first_cell = jnp.arange(GROUPS)[None, :, None] * REG + starts
    first_row = first_cell // GW * TILE
    first_col = first_cell % GW * TILE
    rows_drawn = jax.random.randint(keys[4], (WIN, GROUPS, OWNERS, TR_OWN), 0, 2 * TILE) + first_row[..., None]
    cols_drawn = jax.random.randint(keys[5], (WIN, GROUPS, OWNERS, TR_OWN), 0, 2 * TILE * CAP) + first_col[..., None]
    rows_drawn = jnp.minimum(rows_drawn, TILE * GH - 1)
    cols_drawn = jnp.minimum(cols_drawn, TILE * GW - 1)
    places = jnp.stack([rows_drawn.reshape(WIN, TRACKS), cols_drawn.reshape(WIN, TRACKS)]).astype(jnp.int32)
    return (ids, valid.astype(jnp.int32), places)


def coarse_pair(key):
    base_key = jax.random.fold_in(key, 202)
    keys = jax.random.split(base_key, 2)
    feats = jnp.clip(jax.random.normal(keys[0], (WIN, POS, C), jnp.float32), -6.0, 6.0)
    queries = jnp.clip(jax.random.normal(keys[1], (TRACKS, SUP, C), jnp.float32), -6.0, 6.0)
    return (feats, queries)


def fine_pair(key):
    base_key = jax.random.fold_in(key, 303)
    keys = jax.random.split(base_key, 2)
    tiles = jnp.clip(jax.random.normal(keys[0], (WIN, GROUPS * FT, CELLS, CF), jnp.float32), -6.0, 6.0)
    descs = jnp.clip(jax.random.normal(keys[1], (TRACKS, CF), jnp.float32), -6.0, 6.0)
    return (tiles, descs)


def draw_coarse_query(key, part):
    return coarse_pair(key)[1].astype(jnp.bfloat16)


def draw_coarse_feat(key, part):
    return coarse_pair(key)[0].astype(jnp.bfloat16)


def draw_fine_query(key, part):
    return fine_pair(key)[1].astype(jnp.bfloat16)


def draw_fine_tiles(key, part):
    return fine_pair(key)[0].astype(jnp.bfloat16)


def draw_track_pos(key, part):
    return plan_lists(key)[2]


def draw_tile_list(key, part):
    return plan_lists(key)[0]


def draw_tile_valid(key, part):
    return plan_lists(key)[1]


def setup_inputs(seed: int = 0) -> dict:
    key_list = jax.random.split(jax.random.key(seed), 8)
    coarse_query = draw_coarse_query(jax.random.fold_in(key_list[7], 71), 0)
    coarse_feat = draw_coarse_feat(jax.random.fold_in(key_list[7], 71), 0)
    fine_query = draw_fine_query(jax.random.fold_in(key_list[7], 71), 0)
    fine_tiles = draw_fine_tiles(jax.random.fold_in(key_list[7], 71), 0)
    track_pos = draw_track_pos(jax.random.fold_in(key_list[7], 71), 0)
    tile_list = draw_tile_list(jax.random.fold_in(key_list[7], 71), 0)
    tile_valid = draw_tile_valid(jax.random.fold_in(key_list[7], 71), 0)
    return {"coarse_query": coarse_query, "coarse_feat": coarse_feat, "fine_query": fine_query, "fine_tiles": fine_tiles, "track_pos": track_pos, "tile_list": tile_list, "tile_valid": tile_valid}


spread_cells = 32.0

def refine_frame(descriptors, tile_block, tile_ids, tile_live, track_row, track_col, base_cell):
    slot_count, cell_count, channels = tile_block.shape
    flat_tiles = tile_block.reshape(slot_count * cell_count, channels).astype(jnp.float32)
    scores = jnp.einsum('nc,kc->nk', descriptors.astype(jnp.float32), flat_tiles, precision=lax.Precision.HIGHEST) * (1.0 / math.sqrt(channels))
    global_cell = base_cell + tile_ids.astype(jnp.int32)
    inner_cell = jnp.arange(cell_count, dtype=jnp.int32)
    cell_row = (global_cell // GW * TILE)[:, None] + (inner_cell // TILE)[None, :]
    cell_col = (global_cell % GW * TILE)[:, None] + (inner_cell % TILE)[None, :]
    cell_row = cell_row.reshape(-1).astype(jnp.float32)
    cell_col = cell_col.reshape(-1).astype(jnp.float32)
    distance = (cell_row[None, :] - track_row[:, None]) ** 2 + (cell_col[None, :] - track_col[:, None]) ** 2
    scores = scores - distance * (0.5 / (spread_cells * spread_cells))
    live_cells = jnp.broadcast_to(tile_live[:, None] > 0, (slot_count, cell_count)).reshape(-1)
    scores = jnp.where(live_cells[None, :], scores, -1e+30)
    highest = lax.optimization_barrier(jnp.max(scores, axis=1, keepdims=True))
    weights = jnp.exp(scores - highest)
    totals = lax.optimization_barrier(jnp.sum(weights, axis=1))
    mean_row = lax.optimization_barrier(jnp.sum(weights * cell_row[None, :], axis=1)) / totals
    mean_col = lax.optimization_barrier(jnp.sum(weights * cell_col[None, :], axis=1)) / totals
    return ((mean_row - track_row) / spread_cells, (mean_col - track_col) / spread_cells)

def reference(coarse_query, coarse_feat, fine_query, fine_tiles, track_pos, tile_list, tile_valid):
    track_group = TRACKS // GROUPS
    query_groups = coarse_query.reshape(GROUPS, track_group * SUP, C)
    positions = jnp.arange(POS, dtype=jnp.int32)
    pos_row = (positions // GW).astype(jnp.float32)
    pos_col = (positions % GW).astype(jnp.float32)
    scale = 1.0 / math.sqrt(C)

    def coarse_one(index):
        frame_index = index // GROUPS
        group_index = index % GROUPS
        scores = jnp.dot(query_groups[group_index], coarse_feat[frame_index].T, preferred_element_type=jnp.float32) * scale
        highest = lax.optimization_barrier(jnp.max(scores, axis=1, keepdims=True))
        weights = jnp.exp(scores - highest)
        totals = lax.optimization_barrier(jnp.sum(weights, axis=1))
        row_mean = (lax.optimization_barrier(jnp.sum(weights * pos_row[None, :], axis=1)) / totals).reshape(track_group, SUP).mean(axis=1)
        col_mean = (lax.optimization_barrier(jnp.sum(weights * pos_col[None, :], axis=1)) / totals).reshape(track_group, SUP).mean(axis=1)
        return jnp.stack([(row_mean - (GH - 1) / 2.0) / (GH / 4.0), (col_mean - (GW - 1) / 2.0) / (GW / 4.0)])
    coarse_all = lax.map(coarse_one, jnp.arange(WIN * GROUPS, dtype=jnp.int32))
    coarse_pos = coarse_all.reshape(WIN, GROUPS, 2, track_group).transpose(2, 0, 1, 3).reshape(2, WIN, TRACKS)
    tiles_all = fine_tiles.reshape(WIN, GROUPS, FT, CELLS, CF)
    descs = fine_query.reshape(GROUPS, OWNERS, TR_OWN, CF)
    places = track_pos.astype(jnp.float32).reshape(2, WIN, GROUPS, OWNERS, TR_OWN)
    bases = jnp.arange(GROUPS, dtype=jnp.int32) * REG
    per_owner = jax.vmap(refine_frame, in_axes=(0, 0, 0, 0, 0, 0, None))
    per_group = jax.vmap(per_owner, in_axes=(0, 0, 0, 0, 0, 0, 0))

    def fine_one(frame_index):
        lists = tile_list[frame_index]
        picked = tiles_all[frame_index][jnp.arange(GROUPS, dtype=jnp.int32)[:, None, None], lists]
        rows_out, cols_out = per_group(descs, picked, lists, tile_valid[frame_index], places[0, frame_index], places[1, frame_index], bases)
        return jnp.stack([rows_out, cols_out])
    fine_all = lax.map(fine_one, jnp.arange(WIN, dtype=jnp.int32))
    fine_offset = fine_all.transpose(1, 0, 2, 3, 4).reshape(2, WIN, TRACKS)
    return (coarse_pos, fine_offset)
```

```python
import functools
import math

import jax
import jax.numpy as jnp
from jax import lax
from jax.experimental import pallas as pl
from jax.experimental.pallas import tpu as pltpu
from jax.sharding import PartitionSpec as P

GH = 68
GW = 120
TILE = 8
LOW = -3e38
spread_cells = 32.0

VMEM = pl.BlockSpec(memory_space=pltpu.VMEM)
SMEM = pl.BlockSpec(memory_space=pltpu.SMEM)


def pack_kernel(query_ref, pos_ref, out_ref):
    tracks = query_ref.shape[0]
    window = pos_ref.shape[1]
    lanes = out_ref.shape[1]
    out_ref[...] = jnp.zeros(out_ref.shape, jnp.float32)
    out_ref[0:tracks, :] = query_ref[...].astype(jnp.float32)
    eye = (
        lax.broadcasted_iota(jnp.int32, (window, lanes), 0)
        == lax.broadcasted_iota(jnp.int32, (window, lanes), 1)
    ).astype(jnp.float32)
    for k in range(2):
        out_ref[(k + 1) * tracks : (k + 2) * tracks, :] = lax.dot_general(
            pos_ref[k].astype(jnp.float32),
            eye,
            (((0,), (0,)), ((), ())),
            precision=lax.Precision.HIGHEST,
            preferred_element_type=jnp.float32,
        )


def pack_tracks(fine_query, track_pos):
    return pl.pallas_call(
        pack_kernel,
        out_shape=jax.ShapeDtypeStruct((8, fine_query.shape[1]), jnp.float32),
        in_specs=[VMEM, VMEM],
        out_specs=VMEM,
        name="pack_tracks",
    )(fine_query, track_pos)


def fine_kernel(pieces, own, place_ref, ids_ref, list_ref, valid_ref, tiles_ref, *refs):
    ins, outs = refs[:pieces], refs[pieces:]
    frames, _, cells, channels = tiles_ref.shape
    slots = list_ref.shape[3]
    tracks = pieces * own
    wide = slots * cells
    base = place_ref[0]
    me = place_ref[1]
    scale = 1.0 / math.sqrt(channels)
    query = jnp.concatenate([r[0:own, :] for r in ins], axis=0).astype(jnp.bfloat16)
    rows_in = jnp.concatenate([r[own : 2 * own, :] for r in ins], axis=0)
    cols_in = jnp.concatenate([r[2 * own : 3 * own, :] for r in ins], axis=0)
    lane_in = lax.broadcasted_iota(jnp.int32, (tracks, channels), 1)
    spread = (
        lax.broadcasted_iota(jnp.int32, (slots, wide), 0)
        == lax.broadcasted_iota(jnp.int32, (slots, wide), 1) // cells
    ).astype(jnp.bfloat16)
    inner = lax.broadcasted_iota(jnp.int32, (tracks, wide), 1) % cells
    inner_row = (inner // TILE).astype(jnp.float32)
    inner_col = (inner % TILE).astype(jnp.float32)
    piece_wide = lax.broadcasted_iota(jnp.int32, (tracks, wide), 0) // own
    piece_slot = lax.broadcasted_iota(jnp.int32, (tracks, slots), 0) // own
    lane_out = lax.broadcasted_iota(jnp.int32, (tracks, 2 * frames), 1)
    result = jnp.zeros((tracks, 2 * frames), jnp.float32)
    for i in range(frames):
        scores = jnp.zeros((tracks, wide), jnp.float32)
        codes = jnp.zeros((tracks, slots), jnp.float32)
        for j in range(pieces):
            owner = lax.bitwise_xor(me, j)
            block = jnp.concatenate(
                [tiles_ref[i, ids_ref[i, 0, owner, s]] for s in range(slots)], axis=0
            )
            got = lax.dot_general(
                query, block, (((1,), (1,)), ((), ())), preferred_element_type=jnp.float32
            )
            scores = jnp.where(piece_wide == j, got, scores)
            ids = list_ref[i, 0, pl.ds(owner, 1), :]
            live = valid_ref[i, 0, pl.ds(owner, 1), :]
            code = jnp.where(live > 0, ids, -1).astype(jnp.float32)
            codes = jnp.where(piece_slot == j, jnp.broadcast_to(code, (tracks, slots)), codes)
        code = lax.dot_general(
            codes.astype(jnp.bfloat16),
            spread,
            (((1,), (0,)), ((), ())),
            preferred_element_type=jnp.float32,
        )
        cell = code + base.astype(jnp.float32)
        tile_row = jnp.floor((cell + 0.5) * (1.0 / GW))
        tile_col = cell - GW * tile_row
        here = lane_in == me * frames + i
        track_row = jnp.sum(jnp.where(here, rows_in, 0.0), axis=1, keepdims=True)
        track_col = jnp.sum(jnp.where(here, cols_in, 0.0), axis=1, keepdims=True)
        off_row = (tile_row * TILE + inner_row) - track_row
        off_col = (tile_col * TILE + inner_col) - track_col
        distance = off_row * off_row + off_col * off_col
        scores = scores * scale - distance * (0.5 / (spread_cells * spread_cells))
        scores = jnp.where(code < -0.5, -1e30, scores)
        highest = jnp.max(scores, axis=1, keepdims=True)
        weights = jnp.exp(scores - highest)
        norm = 1.0 / (jnp.sum(weights, axis=1, keepdims=True) * spread_cells)
        mean_row = jnp.sum(weights * off_row, axis=1, keepdims=True) * norm
        mean_col = jnp.sum(weights * off_col, axis=1, keepdims=True) * norm
        result = jnp.where(lane_out == i, mean_row, result)
        result = jnp.where(lane_out == frames + i, mean_col, result)
    eye = (
        lax.broadcasted_iota(jnp.int32, (tracks, tracks), 0)
        == lax.broadcasted_iota(jnp.int32, (tracks, tracks), 1)
    ).astype(jnp.float32)
    turned = lax.dot_general(
        result,
        eye,
        (((0,), (0,)), ((), ())),
        precision=lax.Precision.HIGHEST,
        preferred_element_type=jnp.float32,
    )
    for j in range(pieces):
        for k in range(2):
            outs[j][k] = turned[k * frames : (k + 1) * frames, j * own : (j + 1) * own]


def fine_part(place, tile_list, tile_valid, fine_tiles, own, payloads):
    pieces = len(payloads)
    frames = fine_tiles.shape[0]
    return pl.pallas_call(
        functools.partial(fine_kernel, pieces, own),
        out_shape=[jax.ShapeDtypeStruct((2, frames, own), jnp.float32)] * pieces,
        in_specs=[SMEM, SMEM, VMEM, VMEM, VMEM] + [VMEM] * pieces,
        out_specs=[VMEM] * pieces,
        name="fine_part",
    )(place, tile_list, tile_list, tile_valid, fine_tiles, *payloads)


def coarse_kernel(half, region, place_ref, q_ref, f_ref, *rest):
    if half:
        prev_ref, o_ref, s0, s1 = rest
    else:
        o_ref, s0, s1 = rest
    frames = f_ref.shape[0]
    groups, rows, channels = q_ref.shape
    per = 256 // rows
    quads = groups // per
    steps = frames * quads
    padded = s0.shape[0]
    tiles = padded // 8
    line = GW // 8
    factor = math.log2(math.e) / math.sqrt(channels)
    base = place_ref[0]
    row0 = base // GW
    col0 = base - row0 * GW
    tail = padded - region
    if tail:
        for s in (s0, s1):
            s[padded - 8 : padded, :] = jnp.full((8, 256), LOW, jnp.float32)

    def scores(step, s):
        frame = step // quads
        quad = step % quads
        q = q_ref[pl.ds(quad * per, per)].reshape(256, channels)
        best = jnp.full((8, 256), LOW, jnp.float32)
        for at in range(0, region, 240):
            n = min(240, region - at)
            d = lax.dot_general(
                f_ref[frame, at : at + n, :],
                q,
                (((1,), (1,)), ((), ())),
                preferred_element_type=jnp.float32,
            )
            s[at : at + n, :] = d
            full = n // 8 * 8
            best = jnp.maximum(best, jnp.max(d[:full].reshape(full // 8, 8, 256), axis=0))
        if tail:
            best = jnp.maximum(best, s[padded - 8 : padded, :])
        return jnp.max(best, axis=0, keepdims=True)

    sub = lax.broadcasted_iota(jnp.int32, (8, 128), 0)

    def sums(step, s, best):
        frame = step // quads
        quad = step % quads
        for lt in range(2):
            m = jnp.broadcast_to(best[:, lt * 128 : (lt + 1) * 128], (8, 128))
            cols = [None] * line
            row_sum = jnp.zeros((8, 128), jnp.float32)
            for r in range(pl.cdiv(tiles, line)):
                acc = None
                for j in range(min(line, tiles - r * line)):
                    i = r * line + j
                    p = jnp.exp2((s[8 * i : 8 * i + 8, lt * 128 : (lt + 1) * 128] - m) * factor)
                    cols[j] = p if cols[j] is None else cols[j] + p
                    acc = p if acc is None else acc + p
                if r:
                    row_sum = row_sum + acc * float(r)
            total = None
            col_sum = jnp.zeros((8, 128), jnp.float32)
            for j in range(min(line, tiles)):
                total = cols[j] if total is None else total + cols[j]
                local = sub + (8 * j + col0)
                over = (local >= GW).astype(jnp.float32)
                at = local.astype(jnp.float32) - (GW - 1) / 2.0 - GW * over
                col_sum = col_sum + cols[j] * at
                row_sum = row_sum + cols[j] * over
            row_sum = row_sum + total * (row0.astype(jnp.float32) - (GH - 1) / 2.0)
            stats = [m[0:1]] + [
                jnp.sum(v, axis=0, keepdims=True) for v in (total, row_sum, col_sum)
            ]
            width = min(rows, 128)
            for k in range(128 // width):
                column = lt * 128 + k * width
                group = quad * per + column // rows
                lane = half * rows + column % rows
                for st in range(4):
                    o_ref[
                        group, lane // 128, pl.ds(st * frames + frame, 1), lane % 128 : lane % 128 + width
                    ] = stats[st][:, k * width : (k + 1) * width]

    if half:
        if rows < 128:
            o_ref[:, :, :, 0:rows] = prev_ref[:, :, :, 0:rows]
        else:
            o_ref[:, 0 : rows // 128] = prev_ref[:, 0 : rows // 128]

    def turn(i, best0):
        best1 = scores(2 * i + 1, s1)
        sums(2 * i, s0, best0)
        following = scores(jnp.minimum(2 * i + 2, steps - 1), s0)
        sums(2 * i + 1, s1, best1)
        return following

    lax.fori_loop(0, steps // 2, turn, scores(0, s0))


def coarse_half(place, q, f, prev=None):
    frames, region, channels = f.shape
    groups, rows, _ = q.shape
    half = 0 if prev is None else 1
    padded = pl.cdiv(region, 8) * 8
    return pl.pallas_call(
        functools.partial(coarse_kernel, half, region),
        out_shape=jax.ShapeDtypeStruct((groups, rows // 64, 4 * frames, 128), jnp.float32),
        in_specs=[SMEM, VMEM, VMEM] + [VMEM] * half,
        out_specs=VMEM,
        scratch_shapes=[pltpu.VMEM((padded, 256), jnp.float32)] * 2,
        name=f"coarse_half_{half}",
    )(place, q, f, *([prev] if half else []))


def finish_kernel(pieces, heads, channels, place_ref, stats_ref, *refs):
    scale = math.log2(math.e) / math.sqrt(channels)
    ins, (coarse_ref, fine_ref) = refs[:pieces], refs[pieces:]
    me = place_ref[1]
    sources, tiles, quarter, _ = stats_ref.shape
    frames = quarter // 4
    rows = tiles * 128
    tracks = rows // heads

    def take(d, st):
        return jnp.concatenate(
            [stats_ref[d, t, st * frames : (st + 1) * frames, :] for t in range(tiles)], axis=1
        )

    top = take(0, 0)
    for d in range(1, sources):
        top = jnp.maximum(top, take(d, 0))
    total = jnp.zeros((frames, rows), jnp.float32)
    row = jnp.zeros((frames, rows), jnp.float32)
    col = jnp.zeros((frames, rows), jnp.float32)
    for d in range(sources):
        keep = jnp.exp2((take(d, 0) - top) * scale)
        total = total + take(d, 1) * keep
        row = row + take(d, 2) * keep
        col = col + take(d, 3) * keep
    core = lax.rem(me, 2)
    lane = lax.broadcasted_iota(jnp.int32, (rows, tracks), 0) // heads
    where = lax.broadcasted_iota(jnp.int32, (rows, tracks), 1)
    lane = jnp.where(lane < tracks // 2, lane + core * (tracks // 2), lane - core * (tracks // 2))
    mean = (lane == where).astype(jnp.float32)
    for k, (v, size) in enumerate(((row, GH), (col, GW))):
        coarse_ref[k] = lax.dot_general(
            v / total,
            mean,
            (((1,), (0,)), ((), ())),
            precision=lax.Precision.HIGHEST,
            preferred_element_type=jnp.float32,
        ) * (4.0 / (heads * size))
    for j in range(pieces):
        start = lax.bitwise_xor(me, j) * frames
        for k in range(2):
            fine_ref[k, pl.ds(start, frames), :] = ins[j][k]


def finish(place, stats, pieces, heads, channels, window):
    quarter = stats.shape[2]
    rows = stats.shape[1] * 128
    return pl.pallas_call(
        functools.partial(finish_kernel, len(pieces), heads, channels),
        out_shape=[
            jax.ShapeDtypeStruct((2, quarter // 4, rows // heads), jnp.float32),
            jax.ShapeDtypeStruct((2, window, pieces[0].shape[2]), jnp.float32),
        ],
        in_specs=[SMEM, VMEM] + [VMEM] * len(pieces),
        out_specs=[VMEM, VMEM],
        name="finish",
    )(place, stats, *pieces)


def body(coarse_query, coarse_feat, fine_query, fine_tiles, track_pos, tile_list, tile_valid):
    tracks, heads, channels = coarse_query.shape
    blocks = lax.axis_size("blk")
    owners = lax.axis_size("frames")
    region = coarse_feat.shape[1]
    window = track_pos.shape[1]
    own = fine_query.shape[0]
    me = lax.axis_index("frames").astype(jnp.int32)
    base = lax.axis_index("blk").astype(jnp.int32) * region
    place = jnp.stack([base, me])

    def swap(x, j):
        return lax.ppermute(x, "frames", [(i, i ^ j) for i in range(owners)])

    halves = coarse_query.reshape(2, tracks * heads // 2, channels)
    mine = lax.dynamic_index_in_dim(halves, lax.rem(me, 2), 0, keepdims=True)
    mine = jnp.broadcast_to(mine, (blocks,) + mine.shape[1:])
    first = lax.all_to_all(mine, "blk", split_axis=0, concat_axis=0, tiled=True)

    payload = pack_tracks(fine_query, track_pos)
    payloads = [payload] + [swap(payload, j) for j in range(1, owners)]
    fine = fine_part(place, tile_list, tile_valid, fine_tiles, own, payloads)
    fine = [fine[0]] + [swap(fine[j], j) for j in range(1, owners)]

    second = swap(first, 1)
    stats = coarse_half(place, first, coarse_feat)
    stats = coarse_half(place, second, coarse_feat, stats)
    stats = lax.all_to_all(stats, "blk", split_axis=0, concat_axis=0, tiled=True)
    return tuple(finish(place, stats, fine, heads, channels, window))


def solution(mesh):
    return jax.shard_map(
        body,
        mesh=mesh,
        in_specs=(
            P("blk", None, None),
            P("frames", "blk", None),
            P(("blk", "frames"), None),
            P("frames", "blk", None, None),
            P(None, None, ("blk", "frames")),
            P("frames", "blk", None, None),
            P("frames", "blk", None, None),
        ),
        out_specs=(P(None, "frames", "blk"), P(None, None, ("blk", "frames"))),
        check_vma=False,
    )
```

```python
import functools
import math

import jax
import jax.numpy as jnp
from jax import lax
from jax.experimental import pallas as pl
from jax.experimental.pallas import tpu as pltpu
from jax.sharding import PartitionSpec as P


GH = 68
GW = 120
TILE = 8
LOW = -3e38
spread_cells = 32.0

VMEM = pl.BlockSpec(memory_space=pltpu.VMEM)
SMEM = pl.BlockSpec(memory_space=pltpu.SMEM)
ANY = pl.BlockSpec(memory_space=pl.ANY)
SMALL = pltpu.CompilerParams(vmem_limit_bytes=8 << 20)
LARGE = pltpu.CompilerParams(vmem_limit_bytes=16 << 20)


def pack_kernel(query_ref, pos_ref, out_ref):
    tracks = query_ref.shape[0]
    window = pos_ref.shape[2]
    out_ref[...] = jnp.zeros(out_ref.shape, jnp.float32)
    out_ref[0:tracks, :] = query_ref[...].astype(jnp.float32)
    for k in range(2):
        out_ref[(k + 1) * tracks : (k + 2) * tracks, 0:window] = pos_ref[k].astype(jnp.float32)


def pack_tracks(fine_query, places):
    return pl.pallas_call(
        pack_kernel,
        out_shape=jax.ShapeDtypeStruct((8, fine_query.shape[1]), jnp.float32),
        in_specs=[VMEM, VMEM],
        out_specs=VMEM,
        compiler_params=SMALL,
        name="pack_tracks",
    )(fine_query, places)


def fine_kernel(pieces, own, region, ids_ref, list_ref, valid_ref, tiles_ref, *refs):
    ins, outs = refs[:pieces], refs[pieces:]
    frames, _, cells, channels = tiles_ref.shape
    slots = list_ref.shape[3]
    tracks = pieces * own
    wide = slots * cells
    base = lax.axis_index("blk") * region
    me = lax.axis_index("frames")
    window = outs[0].shape[2]
    scale = 1.0 / math.sqrt(channels)
    query = jnp.concatenate([r[0:own, :] for r in ins], axis=0).astype(jnp.bfloat16)
    rows_in = jnp.concatenate([r[own : 2 * own, :] for r in ins], axis=0)
    cols_in = jnp.concatenate([r[2 * own : 3 * own, :] for r in ins], axis=0)
    lane_in = lax.broadcasted_iota(jnp.int32, (tracks, channels), 1)
    spread = (
        lax.broadcasted_iota(jnp.int32, (slots, wide), 0)
        == lax.broadcasted_iota(jnp.int32, (slots, wide), 1) // cells
    ).astype(jnp.bfloat16)
    inner = lax.broadcasted_iota(jnp.int32, (tracks, wide), 1) % cells
    inner_row = (inner // TILE).astype(jnp.float32)
    inner_col = (inner % TILE).astype(jnp.float32)
    piece_wide = lax.broadcasted_iota(jnp.int32, (tracks, wide), 0) // own
    piece_slot = lax.broadcasted_iota(jnp.int32, (tracks, slots), 0) // own
    lane_out = lax.broadcasted_iota(jnp.int32, (tracks, window), 1)
    rows_out = jnp.zeros((tracks, window), jnp.float32)
    cols_out = jnp.zeros((tracks, window), jnp.float32)
    for i in range(frames):
        scores = jnp.zeros((tracks, wide), jnp.float32)
        codes = jnp.zeros((tracks, slots), jnp.float32)
        for j in range(pieces):
            owner = lax.bitwise_xor(me, j)
            block = jnp.concatenate(
                [tiles_ref[i, ids_ref[i, 0, owner, s]] for s in range(slots)], axis=0
            )
            got = lax.dot_general(
                query, block, (((1,), (1,)), ((), ())), preferred_element_type=jnp.float32
            )
            scores = jnp.where(piece_wide == j, got, scores)
            ids = list_ref[i, 0, pl.ds(owner, 1), :]
            live = valid_ref[i, 0, pl.ds(owner, 1), :]
            code = jnp.where(live > 0, ids, -1).astype(jnp.float32)
            codes = jnp.where(piece_slot == j, jnp.broadcast_to(code, (tracks, slots)), codes)
        code = lax.dot_general(
            codes.astype(jnp.bfloat16),
            spread,
            (((1,), (0,)), ((), ())),
            preferred_element_type=jnp.float32,
        )
        cell = code + base.astype(jnp.float32)
        tile_row = jnp.floor((cell + 0.5) * (1.0 / GW))
        tile_col = cell - GW * tile_row
        here = lane_in == me * frames + i
        track_row = jnp.sum(jnp.where(here, rows_in, 0.0), axis=1, keepdims=True)
        track_col = jnp.sum(jnp.where(here, cols_in, 0.0), axis=1, keepdims=True)
        off_row = (tile_row * TILE + inner_row) - track_row
        off_col = (tile_col * TILE + inner_col) - track_col
        distance = off_row * off_row + off_col * off_col
        scores = scores * scale - distance * (0.5 / (spread_cells * spread_cells))
        scores = jnp.where(code < -0.5, -1e30, scores)
        highest = jnp.max(scores, axis=1, keepdims=True)
        weights = jnp.exp(scores - highest)
        norm = 1.0 / (jnp.sum(weights, axis=1, keepdims=True) * spread_cells)
        mean_row = jnp.sum(weights * off_row, axis=1, keepdims=True) * norm
        mean_col = jnp.sum(weights * off_col, axis=1, keepdims=True) * norm
        rows_out = jnp.where(lane_out == me * frames + i, mean_row, rows_out)
        cols_out = jnp.where(lane_out == me * frames + i, mean_col, cols_out)
    for j in range(pieces):
        outs[j][0] = rows_out[j * own : (j + 1) * own]
        outs[j][1] = cols_out[j * own : (j + 1) * own]


def fine_part(tile_list, tile_valid, fine_tiles, own, window, region, payloads):
    pieces = len(payloads)
    return pl.pallas_call(
        functools.partial(fine_kernel, pieces, own, region),
        out_shape=[jax.ShapeDtypeStruct((2, own, window), jnp.float32)] * pieces,
        in_specs=[SMEM, VMEM, VMEM, VMEM] + [VMEM] * pieces,
        out_specs=[VMEM] * pieces,
        compiler_params=LARGE,
        name="fine_part",
    )(tile_list, tile_list, tile_valid, fine_tiles, *payloads)


def coarse_kernel(half, q_ref, f_ref, gate_ref, *rest):
    if half:
        prev_ref, o_ref, s_ref = rest
    else:
        o_ref, s_ref = rest
    region, frames, channels = f_ref.shape
    groups, rows, _ = q_ref.shape
    per = 256 // rows
    quads = groups // per
    cells = 8 // frames
    run = 15
    seg = run * cells
    factor = math.log2(math.e) / math.sqrt(channels)
    base = lax.axis_index("blk") * region
    sub = lax.broadcasted_iota(jnp.int32, (8, 128), 0)
    inside = (sub // frames).astype(jnp.float32)
    width = min(rows, 128)

    def fold(x):
        y = x
        for k in range(1, cells):
            y = y + pltpu.roll(x, k * frames, 0)
        return y

    def score(quad, at, n):
        q = q_ref[pl.ds(quad * per, per)].reshape(256, channels)
        block = f_ref[pl.ds(at, n)].reshape(n * frames, channels)
        return lax.dot_general(
            block, q, (((1,), (1,)), ((), ())), preferred_element_type=jnp.float32
        )

    def gather(d, at, n, tops, sums):
        out = []
        for lt in range(2):
            total, ramp, row_sum, col_sum = sums[lt]
            for k in range(n // seg):
                acc = None
                for j in range(run):
                    i = k * run + j
                    x = d[8 * i : 8 * i + 8, lt * 128 : (lt + 1) * 128]
                    if tops is not None:
                        x = x - tops[lt]
                    p = jnp.exp2(x * factor)
                    acc = p if acc is None else acc + p
                    ramp = ramp + acc
                first = base + (at + k * seg)
                row = first // GW
                col = first - row * GW
                total = total + acc
                row_sum = row_sum + acc * (row.astype(jnp.float32) - (GH - 1) / 2.0)
                col_sum = col_sum + acc * (col.astype(jnp.float32) - (GW - 1) / 2.0)
            out.append((total, ramp, row_sum, col_sum))
        return out

    zero = jnp.zeros((8, 128), jnp.float32)

    def store(quad, lt, top, sums):
        total, ramp, row_sum, col_sum = sums
        col_sum = col_sum + (run * total - ramp) * float(cells) + total * inside
        total = fold(total)
        for k in range(128 // width):
            column = lt * 128 + k * width
            group = quad * per + column // rows
            lane = half * rows + column % rows
            for st, v in enumerate((top, total, fold(row_sum), fold(col_sum))):
                o_ref[
                    group, lane // 128, st * frames : (st + 1) * frames, lane % 128 : lane % 128 + width
                ] = v[0:frames, k * width : (k + 1) * width]
        return total

    if half:
        if rows < 128:
            o_ref[:, :, :, 0:rows] = prev_ref[:, :, :, 0:rows]
        else:
            o_ref[:, 0 : rows // 128] = prev_ref[:, 0 : rows // 128]

    def plain(quad, worst):
        sums = [(zero, zero, zero, zero)] * 2
        for at in range(0, region, 4 * run):
            n = min(4 * run, region - at)
            sums = gather(score(quad, at, n), at, n, None, sums)
        for lt in range(2):
            total = store(quad, lt, zero, sums[lt])
            good = (total >= 2.0**-90) & (total <= 2.0**100)
            worst = jnp.maximum(worst, jnp.where(good, 0.0, 1.0))
        return worst

    worst = lax.fori_loop(0, quads, plain, zero)

    @pl.when(jnp.max(worst) > 0.0)
    def _():
        chunks = region // seg

        def careful(quad, carry):
            def first(c, best):
                d = score(quad, c * seg, seg)
                s_ref[c] = d
                return jnp.maximum(best, jnp.max(d.reshape(run, 8, 256), axis=0))

            best = lax.fori_loop(0, chunks, first, jnp.full((8, 256), LOW, jnp.float32))
            tops = []
            for lt in range(2):
                top = best[:, lt * 128 : (lt + 1) * 128]
                full = top
                for k in range(1, cells):
                    full = jnp.maximum(full, pltpu.roll(top, k * frames, 0))
                tops.append(full)

            def second(c, sums):
                return gather(s_ref[c], c * seg, seg, tops, sums)

            sums = lax.fori_loop(0, chunks, second, [(zero, zero, zero, zero)] * 2)
            for lt in range(2):
                store(quad, lt, tops[lt], sums[lt])
            return carry

        lax.fori_loop(0, quads, careful, 0)


def coarse_half(q, f, gate, prev=None):
    region, frames, _ = f.shape
    groups, rows, _ = q.shape
    half = 0 if prev is None else 1
    seg = 15 * (8 // frames)
    return pl.pallas_call(
        functools.partial(coarse_kernel, half),
        out_shape=jax.ShapeDtypeStruct((groups, rows // 64, 4 * frames, 128), jnp.float32),
        in_specs=[VMEM, VMEM, ANY] + [VMEM] * half,
        out_specs=VMEM,
        scratch_shapes=[pltpu.VMEM((region // seg, seg * frames, 256), jnp.float32)],
        compiler_params=LARGE,
    )(q, f, gate, *([prev] if half else []))


def finish_kernel(pieces, heads, channels, stats_ref, *refs):
    scale = math.log2(math.e) / math.sqrt(channels)
    ins, (coarse_ref, fine_ref) = refs[:pieces], refs[pieces:]
    me = lax.axis_index("frames")
    sources, tiles, quarter, _ = stats_ref.shape
    frames = quarter // 4
    rows = tiles * 128
    tracks = rows // heads

    def take(d, st):
        return jnp.concatenate(
            [stats_ref[d, t, st * frames : (st + 1) * frames, :] for t in range(tiles)], axis=1
        )

    top = take(0, 0)
    for d in range(1, sources):
        top = jnp.maximum(top, take(d, 0))
    total = jnp.zeros((frames, rows), jnp.float32)
    row = jnp.zeros((frames, rows), jnp.float32)
    col = jnp.zeros((frames, rows), jnp.float32)
    for d in range(sources):
        keep = jnp.exp2((take(d, 0) - top) * scale)
        total = total + take(d, 1) * keep
        row = row + take(d, 2) * keep
        col = col + take(d, 3) * keep
    core = lax.rem(me, 2)
    lane = lax.broadcasted_iota(jnp.int32, (rows, tracks), 0) // heads
    where = lax.broadcasted_iota(jnp.int32, (rows, tracks), 1)
    lane = jnp.where(lane < tracks // 2, lane + core * (tracks // 2), lane - core * (tracks // 2))
    mean = (lane == where).astype(jnp.float32)
    for k, (v, size) in enumerate(((row, GH), (col, GW))):
        coarse_ref[k] = lax.dot_general(
            v / total,
            mean,
            (((1,), (0,)), ((), ())),
            precision=lax.Precision.HIGHEST,
            preferred_element_type=jnp.float32,
        ) * (4.0 / (heads * size))
    for k in range(2):
        fine = ins[0][k]
        for j in range(1, pieces):
            fine = fine + ins[j][k]
        fine_ref[k] = fine


def finish(stats, pieces, heads, channels):
    quarter = stats.shape[2]
    rows = stats.shape[1] * 128
    return pl.pallas_call(
        functools.partial(finish_kernel, len(pieces), heads, channels),
        out_shape=[
            jax.ShapeDtypeStruct((2, quarter // 4, rows // heads), jnp.float32),
            jax.ShapeDtypeStruct(pieces[0].shape, jnp.float32),
        ],
        in_specs=[VMEM] * (1 + len(pieces)),
        out_specs=[VMEM, VMEM],
        compiler_params=SMALL,
        name="finish",
    )(stats, *pieces)


def body(coarse_query, coarse_feat, fine_query, fine_tiles, track_pos, tile_list, tile_valid):
    tracks, heads, channels = coarse_query.shape
    blocks = lax.axis_size("blk")
    owners = lax.axis_size("frames")
    region = coarse_feat.shape[1]
    window = track_pos.shape[1]
    own = fine_query.shape[0]
    me = lax.axis_index("frames").astype(jnp.int32)

    def swap(x, j):
        return lax.ppermute(x, "frames", [(i, i ^ j) for i in range(owners)])

    halves = coarse_query.reshape(2, tracks * heads // 2, channels)
    mine = lax.dynamic_index_in_dim(halves, lax.rem(me, 2), 0, keepdims=True)
    mine = jnp.broadcast_to(mine, (blocks,) + mine.shape[1:])
    first = lax.all_to_all(mine, "blk", split_axis=0, concat_axis=0, tiled=True)

    payload = pack_tracks(fine_query, jnp.transpose(track_pos, (0, 2, 1)))
    payloads = [payload] + [swap(payload, j) for j in range(1, owners)]
    fine = fine_part(tile_list, tile_valid, fine_tiles, own, window, region, payloads)
    gate = fine[0]
    fine = [fine[0]] + [swap(fine[j], j) for j in range(1, owners)]

    cells = jnp.transpose(coarse_feat, (1, 0, 2))
    second = swap(first, 1)
    stats = coarse_half(first, cells, gate)
    stats = coarse_half(second, cells, gate, stats)
    stats = lax.all_to_all(stats, "blk", split_axis=0, concat_axis=0, tiled=True)
    coarse_pos, fine_offset = finish(stats, fine, heads, channels)
    return coarse_pos, jnp.transpose(fine_offset, (0, 2, 1))


def solution(mesh):
    return jax.shard_map(
        body,
        mesh=mesh,
        in_specs=(
            P("blk", None, None),
            P("frames", "blk", None),
            P(("blk", "frames"), None),
            P("frames", "blk", None, None),
            P(None, None, ("blk", "frames")),
            P("frames", "blk", None, None),
            P("frames", "blk", None, None),
        ),
        out_specs=(P(None, "frames", "blk"), P(None, None, ("blk", "frames"))),
        check_vma=False,
    )
```

```python
import functools
import math

import jax
import jax.numpy as jnp
from jax import lax
from jax.experimental import pallas as pl
from jax.experimental.pallas import tpu as pltpu
from jax.sharding import PartitionSpec as P


GH = 68
GW = 120
TILE = 8
LOW = -3e38
spread_cells = 32.0


VMEM = pl.BlockSpec(memory_space=pltpu.VMEM)
SMEM = pl.BlockSpec(memory_space=pltpu.SMEM)
ANY = pl.BlockSpec(memory_space=pl.ANY)
HBM = pl.BlockSpec(memory_space=pltpu.HBM)
SMALL = pltpu.CompilerParams(vmem_limit_bytes=8 << 20)
LARGE = pltpu.CompilerParams(vmem_limit_bytes=16 << 20)


def stay(x):
    return pltpu.with_memory_space_constraint(x, pltpu.HBM)


def prepare_kernel(halves_ref, query_ref, pos_ref, mine_ref, pack_ref, half, query, pos, sems):
    core = lax.rem(lax.axis_index("frames"), 2)
    copies = [
        pltpu.make_async_copy(src, dst, sems.at[k])
        for k, (src, dst) in enumerate(
            ((halves_ref.at[core], half), (query_ref, query), (pos_ref, pos))
        )
    ]
    for copy in copies:
        copy.start()
    for copy in copies:
        copy.wait()
    for k in range(mine_ref.shape[0]):
        mine_ref[k] = half[...]
    tracks = query.shape[0]
    window = pos.shape[2]
    pack_ref[...] = jnp.zeros(pack_ref.shape, jnp.float32)
    pack_ref[0:tracks, :] = query[...].astype(jnp.float32)
    for k in range(2):
        pack_ref[(k + 1) * tracks : (k + 2) * tracks, 0:window] = pos[k].astype(jnp.float32)


def prepare(blocks, halves, fine_query, places):
    _, rows, channels = halves.shape
    return pl.pallas_call(
        prepare_kernel,
        out_shape=[
            jax.ShapeDtypeStruct((blocks, rows, channels), halves.dtype),
            jax.ShapeDtypeStruct((8, fine_query.shape[1]), jnp.float32),
        ],
        in_specs=[HBM] * 3,
        out_specs=[VMEM] * 2,
        scratch_shapes=[
            pltpu.VMEM((rows, channels), halves.dtype),
            pltpu.VMEM(fine_query.shape, fine_query.dtype),
            pltpu.VMEM(places.shape, places.dtype),
            pltpu.SemaphoreType.DMA((3,)),
        ],
        compiler_params=SMALL,
        name="prepare",
    )(*(stay(x) for x in (halves, fine_query, places)))


def fetch_kernel(pieces, own, ids_ref, list_ref, valid_ref, tiles_ref, out_ref, codes_ref, ids, live, sems):
    frames, _, slots = out_ref.shape[:3]
    me = lax.axis_index("frames")
    copies = [
        pltpu.make_async_copy(list_ref, ids, sems.at[frames]),
        pltpu.make_async_copy(valid_ref, live, sems.at[frames + 1]),
    ]
    for copy in copies:
        copy.start()
    for i in range(frames):
        for j in range(pieces):
            for s in range(slots):
                tile = ids_ref[i, 0, lax.bitwise_xor(me, j), s]
                pltpu.make_async_copy(
                    tiles_ref.at[i, tile], out_ref.at[i, j, s], sems.at[i]
                ).start()
    for copy in copies:
        copy.wait()
    for i in range(frames):
        for j in range(pieces):
            owner = lax.bitwise_xor(me, j)
            code = jnp.where(
                live[i, 0, pl.ds(owner, 1), :] > 0, ids[i, 0, pl.ds(owner, 1), :], -1
            ).astype(jnp.float32)
            for k in range(own):
                row = (i * pieces + j) * own + k
                codes_ref[row : row + 1, :] = code
    for i in range(frames):
        pltpu.make_async_copy(out_ref.at[i], out_ref.at[i], sems.at[i]).wait()


def fetch(tile_list, tile_valid, fine_tiles, pieces, own):
    frames, _, cells, channels = fine_tiles.shape
    slots = tile_list.shape[3]
    return pl.pallas_call(
        functools.partial(fetch_kernel, pieces, own),
        out_shape=[
            jax.ShapeDtypeStruct((frames, pieces, slots, cells, channels), fine_tiles.dtype),
            jax.ShapeDtypeStruct((frames * pieces * own, slots), jnp.float32),
        ],
        in_specs=[SMEM, HBM, HBM, HBM],
        out_specs=[VMEM] * 2,
        scratch_shapes=[
            pltpu.VMEM(tile_list.shape, tile_list.dtype),
            pltpu.VMEM(tile_valid.shape, tile_valid.dtype),
            pltpu.SemaphoreType.DMA((frames + 2,)),
        ],
        compiler_params=SMALL,
        name="fetch",
    )(tile_list, *(stay(x) for x in (tile_list, tile_valid, fine_tiles)))


def fine_kernel(pieces, own, region, codes_ref, tiles_ref, *refs):
    ins, outs = refs[:pieces], refs[pieces:]
    frames, _, slots, cells, channels = tiles_ref.shape
    tracks = pieces * own
    wide = slots * cells
    base = lax.axis_index("blk") * region
    me = lax.axis_index("frames")
    window = outs[0].shape[2]
    scale = 1.0 / math.sqrt(channels)
    query = jnp.concatenate([r[0:own, :] for r in ins], axis=0).astype(jnp.bfloat16)
    rows_in = jnp.concatenate([r[own : 2 * own, :] for r in ins], axis=0)
    cols_in = jnp.concatenate([r[2 * own : 3 * own, :] for r in ins], axis=0)
    lane_in = lax.broadcasted_iota(jnp.int32, (tracks, channels), 1)
    spread = (
        lax.broadcasted_iota(jnp.int32, (slots, wide), 0)
        == lax.broadcasted_iota(jnp.int32, (slots, wide), 1) // cells
    ).astype(jnp.bfloat16)
    inner = lax.broadcasted_iota(jnp.int32, (tracks, wide), 1) % cells
    inner_row = (inner // TILE).astype(jnp.float32)
    inner_col = (inner % TILE).astype(jnp.float32)
    piece = lax.broadcasted_iota(jnp.int32, (tracks, wide), 0) // own
    lane_out = lax.broadcasted_iota(jnp.int32, (tracks, window), 1)
    rows_out = jnp.zeros((tracks, window), jnp.float32)
    cols_out = jnp.zeros((tracks, window), jnp.float32)
    codes = lax.dot_general(
        codes_ref[...].astype(jnp.bfloat16),
        spread,
        (((1,), (0,)), ((), ())),
        preferred_element_type=jnp.float32,
    )
    for i in range(frames):
        scores = None
        for j in range(pieces):
            got = lax.dot_general(
                query,
                tiles_ref[i, j].reshape(wide, channels),
                (((1,), (1,)), ((), ())),
                preferred_element_type=jnp.float32,
            )
            scores = got if scores is None else jnp.where(piece == j, got, scores)
        code = codes[i * tracks : (i + 1) * tracks]
        cell = code + base.astype(jnp.float32)
        tile_row = jnp.floor((cell + 0.5) * (1.0 / GW))
        tile_col = cell - GW * tile_row
        here = lane_in == me * frames + i
        track_row = jnp.sum(jnp.where(here, rows_in, 0.0), axis=1, keepdims=True)
        track_col = jnp.sum(jnp.where(here, cols_in, 0.0), axis=1, keepdims=True)
        off_row = (tile_row * TILE + inner_row) - track_row
        off_col = (tile_col * TILE + inner_col) - track_col
        distance = off_row * off_row + off_col * off_col
        scores = scores * scale - distance * (0.5 / (spread_cells * spread_cells))
        scores = jnp.where(code < -0.5, -1e30, scores)
        highest = jnp.max(scores, axis=1, keepdims=True)
        weights = jnp.exp(scores - highest)
        norm = 1.0 / (jnp.sum(weights, axis=1, keepdims=True) * spread_cells)
        mean_row = jnp.sum(weights * off_row, axis=1, keepdims=True) * norm
        mean_col = jnp.sum(weights * off_col, axis=1, keepdims=True) * norm
        rows_out = jnp.where(lane_out == me * frames + i, mean_row, rows_out)
        cols_out = jnp.where(lane_out == me * frames + i, mean_col, cols_out)
    for j in range(pieces):
        outs[j][0] = rows_out[j * own : (j + 1) * own]
        outs[j][1] = cols_out[j * own : (j + 1) * own]


def fine_part(codes, tiles, own, window, region, payloads):
    pieces = len(payloads)
    return pl.pallas_call(
        functools.partial(fine_kernel, pieces, own, region),
        out_shape=[jax.ShapeDtypeStruct((2, own, window), jnp.float32)] * pieces,
        in_specs=[VMEM, VMEM] + [VMEM] * pieces,
        out_specs=[VMEM] * pieces,
        compiler_params=SMALL,
        name="fine_part",
    )(codes, tiles, *payloads)


def coarse_kernel(half, q_ref, f_ref, gate_ref, *rest):
    if half:
        prev_ref, o_ref, s_ref = rest
    else:
        o_ref, s_ref = rest
    region, frames, channels = f_ref.shape
    groups, rows, _ = q_ref.shape
    per = 256 // rows
    quads = groups // per
    cells = 8 // frames
    run = 15
    seg = run * cells
    factor = math.log2(math.e) / math.sqrt(channels)
    base = lax.axis_index("blk") * region
    sub = lax.broadcasted_iota(jnp.int32, (8, 128), 0)
    inside = (sub // frames).astype(jnp.float32)
    width = min(rows, 128)

    def fold(x):
        y = x
        for k in range(1, cells):
            y = y + pltpu.roll(x, k * frames, 0)
        return y

    def score(quad, at, n):
        q = q_ref[pl.ds(quad * per, per)].reshape(256, channels)
        block = f_ref[pl.ds(at, n)].reshape(n * frames, channels)
        return lax.dot_general(
            block, q, (((1,), (1,)), ((), ())), preferred_element_type=jnp.float32
        )

    def gather(d, at, n, tops, sums):
        out = []
        for lt in range(2):
            total, ramp, row_sum, col_sum = sums[lt]
            for k in range(n // seg):
                acc = None
                for j in range(run):
                    i = k * run + j
                    x = d[8 * i : 8 * i + 8, lt * 128 : (lt + 1) * 128]
                    if tops is not None:
                        x = x - tops[lt]
                    p = jnp.exp2(x * factor)
                    acc = p if acc is None else acc + p
                    ramp = ramp + acc
                first = base + (at + k * seg)
                row = first // GW
                col = first - row * GW
                total = total + acc
                row_sum = row_sum + acc * (row.astype(jnp.float32) - (GH - 1) / 2.0)
                col_sum = col_sum + acc * (col.astype(jnp.float32) - (GW - 1) / 2.0)
            out.append((total, ramp, row_sum, col_sum))
        return out

    zero = jnp.zeros((8, 128), jnp.float32)

    def store(quad, lt, top, sums):
        total, ramp, row_sum, col_sum = sums
        col_sum = col_sum + (run * total - ramp) * float(cells) + total * inside
        total = fold(total)
        for k in range(128 // width):
            column = lt * 128 + k * width
            group = quad * per + column // rows
            lane = half * rows + column % rows
            for st, v in enumerate((top, total, fold(row_sum), fold(col_sum))):
                o_ref[
                    group, lane // 128, st * frames : (st + 1) * frames, lane % 128 : lane % 128 + width
                ] = v[0:frames, k * width : (k + 1) * width]
        return total

    if half:
        if rows < 128:
            o_ref[:, :, :, 0:rows] = prev_ref[:, :, :, 0:rows]
        else:
            o_ref[:, 0 : rows // 128] = prev_ref[:, 0 : rows // 128]

    def plain(quad, worst):
        sums = [(zero, zero, zero, zero)] * 2
        for at in range(0, region, 4 * run):
            n = min(4 * run, region - at)
            sums = gather(score(quad, at, n), at, n, None, sums)
        for lt in range(2):
            total = store(quad, lt, zero, sums[lt])
            good = (total >= 2.0**-90) & (total <= 2.0**100)
            worst = jnp.maximum(worst, jnp.where(good, 0.0, 1.0))
        return worst

    worst = lax.fori_loop(0, quads, plain, zero)

    @pl.when(jnp.max(worst) > 0.0)
    def _():
        chunks = region // seg

        def careful(quad, carry):
            def first(c, best):
                d = score(quad, c * seg, seg)
                s_ref[c] = d
                return jnp.maximum(best, jnp.max(d.reshape(run, 8, 256), axis=0))

            best = lax.fori_loop(0, chunks, first, jnp.full((8, 256), LOW, jnp.float32))
            tops = []
            for lt in range(2):
                top = best[:, lt * 128 : (lt + 1) * 128]
                full = top
                for k in range(1, cells):
                    full = jnp.maximum(full, pltpu.roll(top, k * frames, 0))
                tops.append(full)

            def second(c, sums):
                return gather(s_ref[c], c * seg, seg, tops, sums)

            sums = lax.fori_loop(0, chunks, second, [(zero, zero, zero, zero)] * 2)
            for lt in range(2):
                store(quad, lt, tops[lt], sums[lt])
            return carry

        lax.fori_loop(0, quads, careful, 0)


def coarse_half(q, f, gate, prev=None):
    region, frames, _ = f.shape
    groups, rows, _ = q.shape
    half = 0 if prev is None else 1
    seg = 15 * (8 // frames)
    return pl.pallas_call(
        functools.partial(coarse_kernel, half),
        out_shape=jax.ShapeDtypeStruct((groups, rows // 64, 4 * frames, 128), jnp.float32),
        in_specs=[VMEM, VMEM, ANY] + [VMEM] * half,
        out_specs=VMEM,
        scratch_shapes=[pltpu.VMEM((region // seg, seg * frames, 256), jnp.float32)],
        compiler_params=LARGE,
    )(q, f, gate, *([prev] if half else []))


def finish_kernel(pieces, heads, channels, stats_ref, *refs):
    scale = math.log2(math.e) / math.sqrt(channels)
    ins, (coarse_ref, fine_ref) = refs[:pieces], refs[pieces:]
    me = lax.axis_index("frames")
    sources, tiles, quarter, _ = stats_ref.shape
    frames = quarter // 4
    rows = tiles * 128
    tracks = rows // heads

    def take(d, st):
        return jnp.concatenate(
            [stats_ref[d, t, st * frames : (st + 1) * frames, :] for t in range(tiles)], axis=1
        )

    top = take(0, 0)
    for d in range(1, sources):
        top = jnp.maximum(top, take(d, 0))
    total = jnp.zeros((frames, rows), jnp.float32)
    row = jnp.zeros((frames, rows), jnp.float32)
    col = jnp.zeros((frames, rows), jnp.float32)
    for d in range(sources):
        keep = jnp.exp2((take(d, 0) - top) * scale)
        total = total + take(d, 1) * keep
        row = row + take(d, 2) * keep
        col = col + take(d, 3) * keep
    core = lax.rem(me, 2)
    lane = lax.broadcasted_iota(jnp.int32, (rows, tracks), 0) // heads
    where = lax.broadcasted_iota(jnp.int32, (rows, tracks), 1)
    lane = jnp.where(lane < tracks // 2, lane + core * (tracks // 2), lane - core * (tracks // 2))
    mean = (lane == where).astype(jnp.float32)
    for k, (v, size) in enumerate(((row, GH), (col, GW))):
        coarse_ref[k] = lax.dot_general(
            v / total,
            mean,
            (((1,), (0,)), ((), ())),
            precision=lax.Precision.HIGHEST,
            preferred_element_type=jnp.float32,
        ) * (4.0 / (heads * size))
    for k in range(2):
        fine = ins[0][k]
        for j in range(1, pieces):
            fine = fine + ins[j][k]
        fine_ref[k] = fine


def finish(stats, pieces, heads, channels):
    quarter = stats.shape[2]
    rows = stats.shape[1] * 128
    return pl.pallas_call(
        functools.partial(finish_kernel, len(pieces), heads, channels),
        out_shape=[
            jax.ShapeDtypeStruct((2, quarter // 4, rows // heads), jnp.float32),
            jax.ShapeDtypeStruct(pieces[0].shape, jnp.float32),
        ],
        in_specs=[VMEM] * (1 + len(pieces)),
        out_specs=[VMEM, VMEM],
        compiler_params=SMALL,
        name="finish",
    )(stats, *pieces)


def body(coarse_query, coarse_feat, fine_query, fine_tiles, track_pos, tile_list, tile_valid):
    tracks, heads, channels = coarse_query.shape
    blocks = lax.axis_size("blk")
    owners = lax.axis_size("frames")
    region = coarse_feat.shape[1]
    window = track_pos.shape[1]
    own = fine_query.shape[0]

    def swap(x, j):
        return lax.ppermute(x, "frames", [(i, i ^ j) for i in range(owners)])

    halves = coarse_query.reshape(2, tracks * heads // 2, channels)
    mine, payload = prepare(blocks, halves, fine_query, jnp.transpose(track_pos, (0, 2, 1)))
    first = lax.all_to_all(mine, "blk", split_axis=0, concat_axis=0, tiled=True)
    payloads = [payload] + [swap(payload, j) for j in range(1, owners)]
    tiles, codes = fetch(tile_list, tile_valid, fine_tiles, owners, own)
    fine = fine_part(codes, tiles, own, window, region, payloads)
    gate = fine[0]
    fine = [fine[0]] + [swap(fine[j], j) for j in range(1, owners)]

    cells = jnp.transpose(coarse_feat, (1, 0, 2))
    second = swap(first, 1)
    stats = coarse_half(first, cells, gate)
    stats = coarse_half(second, cells, gate, stats)
    stats = lax.all_to_all(stats, "blk", split_axis=0, concat_axis=0, tiled=True)
    coarse_pos, fine_offset = finish(stats, fine, heads, channels)
    return coarse_pos, jnp.transpose(fine_offset, (0, 2, 1))


def solution(mesh):
    return jax.shard_map(
        body,
        mesh=mesh,
        in_specs=(
            P("blk", None, None),
            P("frames", "blk", None),
            P(("blk", "frames"), None),
            P("frames", "blk", None, None),
            P(None, None, ("blk", "frames")),
            P("frames", "blk", None, None),
            P("frames", "blk", None, None),
        ),
        out_specs=(P(None, "frames", "blk"), P(None, None, ("blk", "frames"))),
        check_vma=False,
    )
```

```python
import functools
import math

import jax
import jax.numpy as jnp
from jax import lax
from jax.experimental import pallas as pl
from jax.experimental.pallas import tpu as pltpu
from jax.sharding import PartitionSpec as P


GH = 68
GW = 120
TILE = 8
LOW = -3e38
spread_cells = 32.0


VMEM = pl.BlockSpec(memory_space=pltpu.VMEM)
SMEM = pl.BlockSpec(memory_space=pltpu.SMEM)
ANY = pl.BlockSpec(memory_space=pl.ANY)
HBM = pl.BlockSpec(memory_space=pltpu.HBM)
SMALL = pltpu.CompilerParams(vmem_limit_bytes=8 << 20)
LARGE = pltpu.CompilerParams(vmem_limit_bytes=16 << 20)


def stay(x):
    return pltpu.with_memory_space_constraint(x, pltpu.HBM)


def prepare_kernel(halves_ref, query_ref, pos_ref, mine_ref, pack_ref, half, query, pos, sems):
    blocks = mine_ref.shape[0]
    core = lax.rem(lax.axis_index("frames"), 2)
    reads = [
        pltpu.make_async_copy(src, dst, sems.at[k])
        for k, (src, dst) in enumerate(
            ((halves_ref.at[core], half), (query_ref, query), (pos_ref, pos))
        )
    ]
    writes = [pltpu.make_async_copy(half, mine_ref.at[k], sems.at[3 + k]) for k in range(blocks)]
    for copy in reads:
        copy.start()
    reads[0].wait()
    for copy in writes:
        copy.start()
    for copy in reads[1:]:
        copy.wait()
    tracks = query.shape[0]
    window = pos.shape[2]
    pack_ref[...] = jnp.zeros(pack_ref.shape, jnp.float32)
    pack_ref[0:tracks, :] = query[...].astype(jnp.float32)
    for k in range(2):
        pack_ref[(k + 1) * tracks : (k + 2) * tracks, 0:window] = pos[k].astype(jnp.float32)
    for copy in writes:
        copy.wait()


def prepare(blocks, halves, fine_query, places):
    _, rows, channels = halves.shape
    return pl.pallas_call(
        prepare_kernel,
        out_shape=[
            jax.ShapeDtypeStruct((blocks, rows, channels), halves.dtype),
            jax.ShapeDtypeStruct((8, fine_query.shape[1]), jnp.float32),
        ],
        in_specs=[HBM] * 3,
        out_specs=[HBM, VMEM],
        scratch_shapes=[
            pltpu.VMEM((rows, channels), halves.dtype),
            pltpu.VMEM(fine_query.shape, fine_query.dtype),
            pltpu.VMEM(places.shape, places.dtype),
            pltpu.SemaphoreType.DMA((3 + blocks,)),
        ],
        compiler_params=SMALL,
        name="prepare",
    )(*(stay(x) for x in (halves, fine_query, places)))


def fetch_kernel(pieces, own, ids_ref, list_ref, valid_ref, tiles_ref, out_ref, codes_ref, ids, live, sems):
    frames, _, slots = out_ref.shape[:3]
    me = lax.axis_index("frames")
    copies = [
        pltpu.make_async_copy(list_ref, ids, sems.at[frames]),
        pltpu.make_async_copy(valid_ref, live, sems.at[frames + 1]),
    ]
    for copy in copies:
        copy.start()
    for i in range(frames):
        for j in range(pieces):
            for s in range(slots):
                tile = ids_ref[i, 0, lax.bitwise_xor(me, j), s]
                pltpu.make_async_copy(
                    tiles_ref.at[i, tile], out_ref.at[i, j, s], sems.at[i]
                ).start()
    for copy in copies:
        copy.wait()
    for i in range(frames):
        for j in range(pieces):
            owner = lax.bitwise_xor(me, j)
            code = jnp.where(
                live[i, 0, pl.ds(owner, 1), :] > 0, ids[i, 0, pl.ds(owner, 1), :], -1
            ).astype(jnp.float32)
            for k in range(own):
                row = (i * pieces + j) * own + k
                codes_ref[row : row + 1, :] = code
    for i in range(frames):
        pltpu.make_async_copy(out_ref.at[i], out_ref.at[i], sems.at[i]).wait()


def fetch(tile_list, tile_valid, fine_tiles, pieces, own):
    frames, _, cells, channels = fine_tiles.shape
    slots = tile_list.shape[3]
    return pl.pallas_call(
        functools.partial(fetch_kernel, pieces, own),
        out_shape=[
            jax.ShapeDtypeStruct((frames, pieces, slots, cells, channels), fine_tiles.dtype),
            jax.ShapeDtypeStruct((frames * pieces * own, slots), jnp.float32),
        ],
        in_specs=[SMEM, HBM, HBM, HBM],
        out_specs=[VMEM] * 2,
        scratch_shapes=[
            pltpu.VMEM(tile_list.shape, tile_list.dtype),
            pltpu.VMEM(tile_valid.shape, tile_valid.dtype),
            pltpu.SemaphoreType.DMA((frames + 2,)),
        ],
        compiler_params=SMALL,
        name="fetch",
    )(tile_list, *(stay(x) for x in (tile_list, tile_valid, fine_tiles)))


def fine_kernel(pieces, own, region, codes_ref, tiles_ref, *refs):
    ins, outs = refs[:pieces], refs[pieces:]
    frames, _, slots, cells, channels = tiles_ref.shape
    tracks = pieces * own
    wide = slots * cells
    base = lax.axis_index("blk") * region
    me = lax.axis_index("frames")
    window = outs[0].shape[2]
    scale = 1.0 / math.sqrt(channels)
    query = jnp.concatenate([r[0:own, :] for r in ins], axis=0).astype(jnp.bfloat16)
    rows_in = jnp.concatenate([r[own : 2 * own, :] for r in ins], axis=0)
    cols_in = jnp.concatenate([r[2 * own : 3 * own, :] for r in ins], axis=0)
    lane_in = lax.broadcasted_iota(jnp.int32, (tracks, channels), 1)
    spread = (
        lax.broadcasted_iota(jnp.int32, (slots, wide), 0)
        == lax.broadcasted_iota(jnp.int32, (slots, wide), 1) // cells
    ).astype(jnp.bfloat16)
    inner = lax.broadcasted_iota(jnp.int32, (tracks, wide), 1) % cells
    inner_row = (inner // TILE).astype(jnp.float32)
    inner_col = (inner % TILE).astype(jnp.float32)
    piece = lax.broadcasted_iota(jnp.int32, (tracks, wide), 0) // own
    lane_out = lax.broadcasted_iota(jnp.int32, (tracks, window), 1)
    rows_out = jnp.zeros((tracks, window), jnp.float32)
    cols_out = jnp.zeros((tracks, window), jnp.float32)
    codes = lax.dot_general(
        codes_ref[...].astype(jnp.bfloat16),
        spread,
        (((1,), (0,)), ((), ())),
        preferred_element_type=jnp.float32,
    )
    for i in range(frames):
        scores = None
        for j in range(pieces):
            got = lax.dot_general(
                query,
                tiles_ref[i, j].reshape(wide, channels),
                (((1,), (1,)), ((), ())),
                preferred_element_type=jnp.float32,
            )
            scores = got if scores is None else jnp.where(piece == j, got, scores)
        code = codes[i * tracks : (i + 1) * tracks]
        cell = code + base.astype(jnp.float32)
        tile_row = jnp.floor((cell + 0.5) * (1.0 / GW))
        tile_col = cell - GW * tile_row
        here = lane_in == me * frames + i
        track_row = jnp.sum(jnp.where(here, rows_in, 0.0), axis=1, keepdims=True)
        track_col = jnp.sum(jnp.where(here, cols_in, 0.0), axis=1, keepdims=True)
        off_row = (tile_row * TILE + inner_row) - track_row
        off_col = (tile_col * TILE + inner_col) - track_col
        distance = off_row * off_row + off_col * off_col
        scores = scores * scale - distance * (0.5 / (spread_cells * spread_cells))
        scores = jnp.where(code < -0.5, -1e30, scores)
        highest = jnp.max(scores, axis=1, keepdims=True)
        weights = jnp.exp(scores - highest)
        norm = 1.0 / (jnp.sum(weights, axis=1, keepdims=True) * spread_cells)
        mean_row = jnp.sum(weights * off_row, axis=1, keepdims=True) * norm
        mean_col = jnp.sum(weights * off_col, axis=1, keepdims=True) * norm
        rows_out = jnp.where(lane_out == me * frames + i, mean_row, rows_out)
        cols_out = jnp.where(lane_out == me * frames + i, mean_col, cols_out)
    for j in range(pieces):
        outs[j][0] = rows_out[j * own : (j + 1) * own]
        outs[j][1] = cols_out[j * own : (j + 1) * own]


def fine_part(codes, tiles, own, window, region, payloads):
    pieces = len(payloads)
    return pl.pallas_call(
        functools.partial(fine_kernel, pieces, own, region),
        out_shape=[jax.ShapeDtypeStruct((2, own, window), jnp.float32)] * pieces,
        in_specs=[VMEM, VMEM] + [VMEM] * pieces,
        out_specs=[VMEM] * pieces,
        compiler_params=SMALL,
        name="fine_part",
    )(codes, tiles, *payloads)


def coarse_kernel(half, q_ref, f_ref, gate_ref, *rest):
    if half:
        prev_ref, o_ref, s_ref = rest
    else:
        o_ref, s_ref = rest
    region, frames, channels = f_ref.shape
    groups, rows, _ = q_ref.shape
    per = 256 // rows
    quads = groups // per
    cells = 8 // frames
    run = 15
    seg = run * cells
    factor = math.log2(math.e) / math.sqrt(channels)
    base = lax.axis_index("blk") * region
    sub = lax.broadcasted_iota(jnp.int32, (8, 128), 0)
    inside = (sub // frames).astype(jnp.float32)
    width = min(rows, 128)

    def fold(x):
        y = x
        for k in range(1, cells):
            y = y + pltpu.roll(x, k * frames, 0)
        return y

    def score(quad, at, n):
        q = q_ref[pl.ds(quad * per, per)].reshape(256, channels)
        block = f_ref[pl.ds(at, n)].reshape(n * frames, channels)
        return lax.dot_general(
            block, q, (((1,), (1,)), ((), ())), preferred_element_type=jnp.float32
        )

    def gather(d, at, n, tops, sums):
        out = []
        for lt in range(2):
            total, ramp, row_sum, col_sum = sums[lt]
            for k in range(n // seg):
                acc = None
                for j in range(run):
                    i = k * run + j
                    x = d[8 * i : 8 * i + 8, lt * 128 : (lt + 1) * 128]
                    if tops is not None:
                        x = x - tops[lt]
                    p = jnp.exp2(x * factor)
                    acc = p if acc is None else acc + p
                    ramp = ramp + acc
                first = base + (at + k * seg)
                row = first // GW
                col = first - row * GW
                total = total + acc
                row_sum = row_sum + acc * (row.astype(jnp.float32) - (GH - 1) / 2.0)
                col_sum = col_sum + acc * (col.astype(jnp.float32) - (GW - 1) / 2.0)
            out.append((total, ramp, row_sum, col_sum))
        return out

    zero = jnp.zeros((8, 128), jnp.float32)

    def store(quad, lt, top, sums):
        total, ramp, row_sum, col_sum = sums
        col_sum = col_sum + (run * total - ramp) * float(cells) + total * inside
        total = fold(total)
        for k in range(128 // width):
            column = lt * 128 + k * width
            group = quad * per + column // rows
            lane = half * rows + column % rows
            for st, v in enumerate((top, total, fold(row_sum), fold(col_sum))):
                o_ref[
                    group, lane // 128, st * frames : (st + 1) * frames, lane % 128 : lane % 128 + width
                ] = v[0:frames, k * width : (k + 1) * width]
        return total

    if half:
        if rows < 128:
            o_ref[:, :, :, 0:rows] = prev_ref[:, :, :, 0:rows]
        else:
            o_ref[:, 0 : rows // 128] = prev_ref[:, 0 : rows // 128]

    def plain(quad, worst):
        sums = [(zero, zero, zero, zero)] * 2
        for at in range(0, region, 4 * run):
            n = min(4 * run, region - at)
            sums = gather(score(quad, at, n), at, n, None, sums)
        for lt in range(2):
            total = store(quad, lt, zero, sums[lt])
            good = (total >= 2.0**-90) & (total <= 2.0**100)
            worst = jnp.maximum(worst, jnp.where(good, 0.0, 1.0))
        return worst

    worst = lax.fori_loop(0, quads, plain, zero)

    @pl.when(jnp.max(worst) > 0.0)
    def _():
        chunks = region // seg

        def careful(quad, carry):
            def first(c, best):
                d = score(quad, c * seg, seg)
                s_ref[c] = d
                return jnp.maximum(best, jnp.max(d.reshape(run, 8, 256), axis=0))

            best = lax.fori_loop(0, chunks, first, jnp.full((8, 256), LOW, jnp.float32))
            tops = []
            for lt in range(2):
                top = best[:, lt * 128 : (lt + 1) * 128]
                full = top
                for k in range(1, cells):
                    full = jnp.maximum(full, pltpu.roll(top, k * frames, 0))
                tops.append(full)

            def second(c, sums):
                return gather(s_ref[c], c * seg, seg, tops, sums)

            sums = lax.fori_loop(0, chunks, second, [(zero, zero, zero, zero)] * 2)
            for lt in range(2):
                store(quad, lt, tops[lt], sums[lt])
            return carry

        lax.fori_loop(0, quads, careful, 0)


def coarse_half(q, f, gate, prev=None):
    region, frames, _ = f.shape
    groups, rows, _ = q.shape
    half = 0 if prev is None else 1
    seg = 15 * (8 // frames)
    return pl.pallas_call(
        functools.partial(coarse_kernel, half),
        out_shape=jax.ShapeDtypeStruct((groups, rows // 64, 4 * frames, 128), jnp.float32),
        in_specs=[VMEM, VMEM, ANY] + [VMEM] * half,
        out_specs=VMEM,
        scratch_shapes=[pltpu.VMEM((region // seg, seg * frames, 256), jnp.float32)],
        compiler_params=LARGE,
    )(q, f, gate, *([prev] if half else []))


def finish_kernel(pieces, heads, channels, stats_ref, *refs):
    scale = math.log2(math.e) / math.sqrt(channels)
    ins, (coarse_ref, fine_ref) = refs[:pieces], refs[pieces:]
    me = lax.axis_index("frames")
    sources, tiles, quarter, _ = stats_ref.shape
    frames = quarter // 4
    rows = tiles * 128
    tracks = rows // heads

    def take(d, st):
        return jnp.concatenate(
            [stats_ref[d, t, st * frames : (st + 1) * frames, :] for t in range(tiles)], axis=1
        )

    top = take(0, 0)
    for d in range(1, sources):
        top = jnp.maximum(top, take(d, 0))
    total = jnp.zeros((frames, rows), jnp.float32)
    row = jnp.zeros((frames, rows), jnp.float32)
    col = jnp.zeros((frames, rows), jnp.float32)
    for d in range(sources):
        keep = jnp.exp2((take(d, 0) - top) * scale)
        total = total + take(d, 1) * keep
        row = row + take(d, 2) * keep
        col = col + take(d, 3) * keep
    core = lax.rem(me, 2)
    lane = lax.broadcasted_iota(jnp.int32, (rows, tracks), 0) // heads
    where = lax.broadcasted_iota(jnp.int32, (rows, tracks), 1)
    lane = jnp.where(lane < tracks // 2, lane + core * (tracks // 2), lane - core * (tracks // 2))
    mean = (lane == where).astype(jnp.float32)
    for k, (v, size) in enumerate(((row, GH), (col, GW))):
        coarse_ref[k] = lax.dot_general(
            v / total,
            mean,
            (((1,), (0,)), ((), ())),
            precision=lax.Precision.HIGHEST,
            preferred_element_type=jnp.float32,
        ) * (4.0 / (heads * size))
    for k in range(2):
        fine = ins[0][k]
        for j in range(1, pieces):
            fine = fine + ins[j][k]
        fine_ref[k] = fine


def finish(stats, pieces, heads, channels):
    quarter = stats.shape[2]
    rows = stats.shape[1] * 128
    return pl.pallas_call(
        functools.partial(finish_kernel, len(pieces), heads, channels),
        out_shape=[
            jax.ShapeDtypeStruct((2, quarter // 4, rows // heads), jnp.float32),
            jax.ShapeDtypeStruct(pieces[0].shape, jnp.float32),
        ],
        in_specs=[VMEM] * (1 + len(pieces)),
        out_specs=[VMEM, VMEM],
        compiler_params=SMALL,
        name="finish",
    )(stats, *pieces)


def body(coarse_query, coarse_feat, fine_query, fine_tiles, track_pos, tile_list, tile_valid):
    tracks, heads, channels = coarse_query.shape
    blocks = lax.axis_size("blk")
    owners = lax.axis_size("frames")
    region = coarse_feat.shape[1]
    window = track_pos.shape[1]
    own = fine_query.shape[0]

    def swap(x, j):
        return lax.ppermute(x, "frames", [(i, i ^ j) for i in range(owners)])

    halves = coarse_query.reshape(2, tracks * heads // 2, channels)
    mine, payload = prepare(blocks, halves, fine_query, jnp.transpose(track_pos, (0, 2, 1)))
    first = lax.all_to_all(mine, "blk", split_axis=0, concat_axis=0, tiled=True)
    payloads = [payload] + [swap(payload, j) for j in range(1, owners)]
    tiles, codes = fetch(tile_list, tile_valid, fine_tiles, owners, own)
    fine = fine_part(codes, tiles, own, window, region, payloads)
    gate = fine[0]
    fine = [fine[0]] + [swap(fine[j], j) for j in range(1, owners)]

    cells = jnp.transpose(coarse_feat, (1, 0, 2))
    second = swap(first, 1)
    stats = coarse_half(first, cells, gate)
    stats = coarse_half(second, cells, gate, stats)
    stats = lax.all_to_all(stats, "blk", split_axis=0, concat_axis=0, tiled=True)
    coarse_pos, fine_offset = finish(stats, fine, heads, channels)
    return coarse_pos, jnp.transpose(fine_offset, (0, 2, 1))


def solution(mesh):
    return jax.shard_map(
        body,
        mesh=mesh,
        in_specs=(
            P("blk", None, None),
            P("frames", "blk", None),
            P(("blk", "frames"), None),
            P("frames", "blk", None, None),
            P(None, None, ("blk", "frames")),
            P("frames", "blk", None, None),
            P("frames", "blk", None, None),
        ),
        out_specs=(P(None, "frames", "blk"), P(None, None, ("blk", "frames"))),
        check_vma=False,
    )
```

```python
import functools
import math

import jax
import jax.numpy as jnp
from jax import lax
from jax.experimental import pallas as pl
from jax.experimental.pallas import tpu as pltpu
from jax.sharding import PartitionSpec as P


GH = 68
GW = 120
TILE = 8
LOW = -3e38
spread_cells = 32.0


VMEM = pl.BlockSpec(memory_space=pltpu.VMEM)
SMEM = pl.BlockSpec(memory_space=pltpu.SMEM)
ANY = pl.BlockSpec(memory_space=pl.ANY)
HBM = pl.BlockSpec(memory_space=pltpu.HBM)
SMALL = pltpu.CompilerParams(vmem_limit_bytes=8 << 20)
LARGE = pltpu.CompilerParams(vmem_limit_bytes=16 << 20)


def stay(x):
    return pltpu.with_memory_space_constraint(x, pltpu.HBM)


def prepare_kernel(halves_ref, query_ref, pos_ref, mine_ref, pack_ref, half, query, pos, sems):
    blocks = mine_ref.shape[0]
    core = lax.rem(lax.axis_index("frames"), 2)
    reads = [
        pltpu.make_async_copy(src, dst, sems.at[k])
        for k, (src, dst) in enumerate(
            ((halves_ref.at[core], half), (query_ref, query), (pos_ref, pos))
        )
    ]
    writes = [pltpu.make_async_copy(half, mine_ref.at[k], sems.at[3 + k]) for k in range(blocks)]
    for copy in reads:
        copy.start()
    reads[0].wait()
    for copy in writes:
        copy.start()
    for copy in reads[1:]:
        copy.wait()
    tracks = query.shape[0]
    window = pos.shape[2]
    pack_ref[...] = jnp.zeros(pack_ref.shape, jnp.float32)
    pack_ref[0:tracks, :] = query[...].astype(jnp.float32)
    for k in range(2):
        pack_ref[(k + 1) * tracks : (k + 2) * tracks, 0:window] = pos[k].astype(jnp.float32)
    for copy in writes:
        copy.wait()


def prepare(blocks, halves, fine_query, places):
    _, rows, channels = halves.shape
    return pl.pallas_call(
        prepare_kernel,
        out_shape=[
            jax.ShapeDtypeStruct((blocks, rows, channels), halves.dtype),
            jax.ShapeDtypeStruct((8, fine_query.shape[1]), jnp.float32),
        ],
        in_specs=[HBM] * 3,
        out_specs=[HBM, VMEM],
        scratch_shapes=[
            pltpu.VMEM((rows, channels), halves.dtype),
            pltpu.VMEM(fine_query.shape, fine_query.dtype),
            pltpu.VMEM(places.shape, places.dtype),
            pltpu.SemaphoreType.DMA((3 + blocks,)),
        ],
        compiler_params=SMALL,
        name="prepare",
    )(*(stay(x) for x in (halves, fine_query, places)))


def fetch_kernel(pieces, own, ids_ref, list_ref, valid_ref, tiles_ref, out_ref, codes_ref, ids, live, sems):
    frames, _, slots = out_ref.shape[:3]
    me = lax.axis_index("frames")
    copies = [
        pltpu.make_async_copy(list_ref, ids, sems.at[frames]),
        pltpu.make_async_copy(valid_ref, live, sems.at[frames + 1]),
    ]
    for copy in copies:
        copy.start()
    for i in range(frames):
        for j in range(pieces):
            for s in range(slots):
                tile = ids_ref[i, 0, lax.bitwise_xor(me, j), s]
                pltpu.make_async_copy(
                    tiles_ref.at[i, tile], out_ref.at[i, j, s], sems.at[i]
                ).start()
    for copy in copies:
        copy.wait()
    for i in range(frames):
        for j in range(pieces):
            owner = lax.bitwise_xor(me, j)
            code = jnp.where(
                live[i, 0, pl.ds(owner, 1), :] > 0, ids[i, 0, pl.ds(owner, 1), :], -1
            ).astype(jnp.float32)
            for k in range(own):
                row = (i * pieces + j) * own + k
                codes_ref[row : row + 1, :] = code
    for i in range(frames):
        pltpu.make_async_copy(out_ref.at[i], out_ref.at[i], sems.at[i]).wait()


def fetch(tile_list, tile_valid, fine_tiles, pieces, own):
    frames, _, cells, channels = fine_tiles.shape
    slots = tile_list.shape[3]
    return pl.pallas_call(
        functools.partial(fetch_kernel, pieces, own),
        out_shape=[
            jax.ShapeDtypeStruct((frames, pieces, slots, cells, channels), fine_tiles.dtype),
            jax.ShapeDtypeStruct((frames * pieces * own, slots), jnp.float32),
        ],
        in_specs=[SMEM, HBM, HBM, HBM],
        out_specs=[VMEM] * 2,
        scratch_shapes=[
            pltpu.VMEM(tile_list.shape, tile_list.dtype),
            pltpu.VMEM(tile_valid.shape, tile_valid.dtype),
            pltpu.SemaphoreType.DMA((frames + 2,)),
        ],
        compiler_params=SMALL,
        name="fetch",
    )(tile_list, *(stay(x) for x in (tile_list, tile_valid, fine_tiles)))


def fine_kernel(pieces, own, region, codes_ref, tiles_ref, *refs):
    ins, outs = refs[:pieces], refs[pieces:]
    frames, _, slots, cells, channels = tiles_ref.shape
    tracks = pieces * own
    wide = slots * cells
    base = lax.axis_index("blk") * region
    me = lax.axis_index("frames")
    window = outs[0].shape[2]
    scale = 1.0 / math.sqrt(channels)
    query = jnp.concatenate([r[0:own, :] for r in ins], axis=0).astype(jnp.bfloat16)
    rows_in = jnp.concatenate([r[own : 2 * own, :] for r in ins], axis=0)
    cols_in = jnp.concatenate([r[2 * own : 3 * own, :] for r in ins], axis=0)
    lane_in = lax.broadcasted_iota(jnp.int32, (tracks, channels), 1)
    spread = (
        lax.broadcasted_iota(jnp.int32, (slots, wide), 0)
        == lax.broadcasted_iota(jnp.int32, (slots, wide), 1) // cells
    ).astype(jnp.bfloat16)
    inner = lax.broadcasted_iota(jnp.int32, (tracks, wide), 1) % cells
    inner_row = (inner // TILE).astype(jnp.float32)
    inner_col = (inner % TILE).astype(jnp.float32)
    piece = lax.broadcasted_iota(jnp.int32, (tracks, wide), 0) // own
    lane_out = lax.broadcasted_iota(jnp.int32, (tracks, window), 1)
    rows_out = jnp.zeros((tracks, window), jnp.float32)
    cols_out = jnp.zeros((tracks, window), jnp.float32)
    codes = lax.dot_general(
        codes_ref[...].astype(jnp.bfloat16),
        spread,
        (((1,), (0,)), ((), ())),
        preferred_element_type=jnp.float32,
    )
    for i in range(frames):
        scores = None
        for j in range(pieces):
            got = lax.dot_general(
                query,
                tiles_ref[i, j].reshape(wide, channels),
                (((1,), (1,)), ((), ())),
                preferred_element_type=jnp.float32,
            )
            scores = got if scores is None else jnp.where(piece == j, got, scores)
        code = codes[i * tracks : (i + 1) * tracks]
        cell = code + base.astype(jnp.float32)
        tile_row = jnp.floor((cell + 0.5) * (1.0 / GW))
        tile_col = cell - GW * tile_row
        here = lane_in == me * frames + i
        track_row = jnp.sum(jnp.where(here, rows_in, 0.0), axis=1, keepdims=True)
        track_col = jnp.sum(jnp.where(here, cols_in, 0.0), axis=1, keepdims=True)
        off_row = (tile_row * TILE + inner_row) - track_row
        off_col = (tile_col * TILE + inner_col) - track_col
        distance = off_row * off_row + off_col * off_col
        scores = scores * scale - distance * (0.5 / (spread_cells * spread_cells))
        scores = jnp.where(code < -0.5, -1e30, scores)
        highest = jnp.max(scores, axis=1, keepdims=True)
        weights = jnp.exp(scores - highest)
        norm = 1.0 / (jnp.sum(weights, axis=1, keepdims=True) * spread_cells)
        mean_row = jnp.sum(weights * off_row, axis=1, keepdims=True) * norm
        mean_col = jnp.sum(weights * off_col, axis=1, keepdims=True) * norm
        rows_out = jnp.where(lane_out == me * frames + i, mean_row, rows_out)
        cols_out = jnp.where(lane_out == me * frames + i, mean_col, cols_out)
    for j in range(pieces):
        outs[j][0] = rows_out[j * own : (j + 1) * own]
        outs[j][1] = cols_out[j * own : (j + 1) * own]


def fine_part(codes, tiles, own, window, region, payloads):
    pieces = len(payloads)
    return pl.pallas_call(
        functools.partial(fine_kernel, pieces, own, region),
        out_shape=[jax.ShapeDtypeStruct((2, own, window), jnp.float32)] * pieces,
        in_specs=[VMEM, VMEM] + [VMEM] * pieces,
        out_specs=[VMEM] * pieces,
        compiler_params=SMALL,
        name="fine_part",
    )(codes, tiles, *payloads)


def coarse_kernel(half, q_ref, f_ref, gate_ref, *rest):
    if half:
        prev_ref, o_ref, s_ref = rest
    else:
        o_ref, s_ref = rest
    region, frames, channels = f_ref.shape
    groups, rows, _ = q_ref.shape
    per = 256 // rows
    quads = groups // per
    cells = 8 // frames
    run = 15
    seg = run * cells
    factor = math.log2(math.e) / math.sqrt(channels)
    base = lax.axis_index("blk") * region
    sub = lax.broadcasted_iota(jnp.int32, (8, 128), 0)
    inside = (sub // frames).astype(jnp.float32)
    width = min(rows, 128)

    def fold(x):
        y = x
        for k in range(1, cells):
            y = y + pltpu.roll(x, k * frames, 0)
        return y

    def score(quad, at, n):
        q = q_ref[pl.ds(quad * per, per)].reshape(256, channels)
        block = f_ref[pl.ds(at, n)].reshape(n * frames, channels)
        return lax.dot_general(
            block, q, (((1,), (1,)), ((), ())), preferred_element_type=jnp.float32
        )

    def gather(d, at, n, tops, sums):
        out = []
        for lt in range(2):
            total, ramp, row_sum, col_sum = sums[lt]
            for k in range(n // seg):
                acc = None
                for j in range(run):
                    i = k * run + j
                    x = d[8 * i : 8 * i + 8, lt * 128 : (lt + 1) * 128]
                    if tops is not None:
                        x = x - tops[lt]
                    p = jnp.exp2(x * factor)
                    acc = p if acc is None else acc + p
                    ramp = ramp + acc
                first = base + (at + k * seg)
                row = first // GW
                col = first - row * GW
                total = total + acc
                row_sum = row_sum + acc * (row.astype(jnp.float32) - (GH - 1) / 2.0)
                col_sum = col_sum + acc * (col.astype(jnp.float32) - (GW - 1) / 2.0)
            out.append((total, ramp, row_sum, col_sum))
        return out

    zero = jnp.zeros((8, 128), jnp.float32)

    def store(quad, lt, top, sums):
        total, ramp, row_sum, col_sum = sums
        col_sum = col_sum + (run * total - ramp) * float(cells) + total * inside
        total = fold(total)
        for k in range(128 // width):
            column = lt * 128 + k * width
            group = quad * per + column // rows
            lane = half * rows + column % rows
            for st, v in enumerate((top, total, fold(row_sum), fold(col_sum))):
                o_ref[
                    group, lane // 128, st * frames : (st + 1) * frames, lane % 128 : lane % 128 + width
                ] = v[0:frames, k * width : (k + 1) * width]
        return total

    if half:
        if rows < 128:
            o_ref[:, :, :, 0:rows] = prev_ref[:, :, :, 0:rows]
        else:
            o_ref[:, 0 : rows // 128] = prev_ref[:, 0 : rows // 128]

    def plain(quad, worst):
        sums = [(zero, zero, zero, zero)] * 2
        for at in range(0, region, 4 * run):
            n = min(4 * run, region - at)
            sums = gather(score(quad, at, n), at, n, None, sums)
        for lt in range(2):
            total = store(quad, lt, zero, sums[lt])
            good = (total >= 2.0**-90) & (total <= 2.0**100)
            worst = jnp.maximum(worst, jnp.where(good, 0.0, 1.0))
        return worst

    worst = lax.fori_loop(0, quads, plain, zero)

    @pl.when(jnp.max(worst) > 0.0)
    def _():
        chunks = region // seg

        def careful(quad, carry):
            def first(c, best):
                d = score(quad, c * seg, seg)
                s_ref[c] = d
                return jnp.maximum(best, jnp.max(d.reshape(run, 8, 256), axis=0))

            best = lax.fori_loop(0, chunks, first, jnp.full((8, 256), LOW, jnp.float32))
            tops = []
            for lt in range(2):
                top = best[:, lt * 128 : (lt + 1) * 128]
                full = top
                for k in range(1, cells):
                    full = jnp.maximum(full, pltpu.roll(top, k * frames, 0))
                tops.append(full)

            def second(c, sums):
                return gather(s_ref[c], c * seg, seg, tops, sums)

            sums = lax.fori_loop(0, chunks, second, [(zero, zero, zero, zero)] * 2)
            for lt in range(2):
                store(quad, lt, tops[lt], sums[lt])
            return carry

        lax.fori_loop(0, quads, careful, 0)


def coarse_half(q, f, gate, prev=None):
    region, frames, _ = f.shape
    groups, rows, _ = q.shape
    half = 0 if prev is None else 1
    seg = 15 * (8 // frames)
    return pl.pallas_call(
        functools.partial(coarse_kernel, half),
        out_shape=jax.ShapeDtypeStruct((groups, rows // 64, 4 * frames, 128), jnp.float32),
        in_specs=[VMEM, VMEM, ANY] + [VMEM] * half,
        out_specs=VMEM,
        scratch_shapes=[pltpu.VMEM((region // seg, seg * frames, 256), jnp.float32)],
        compiler_params=LARGE,
    )(q, f, gate, *([prev] if half else []))


def finish_kernel(pieces, heads, channels, stats_ref, *refs):
    scale = math.log2(math.e) / math.sqrt(channels)
    ins, (coarse_ref, fine_ref) = refs[:pieces], refs[pieces:]
    me = lax.axis_index("frames")
    sources, tiles, quarter, _ = stats_ref.shape
    frames = quarter // 4
    rows = tiles * 128
    tracks = rows // heads

    def take(d, st):
        return jnp.concatenate(
            [stats_ref[d, t, st * frames : (st + 1) * frames, :] for t in range(tiles)], axis=1
        )

    top = take(0, 0)
    for d in range(1, sources):
        top = jnp.maximum(top, take(d, 0))
    total = jnp.zeros((frames, rows), jnp.float32)
    row = jnp.zeros((frames, rows), jnp.float32)
    col = jnp.zeros((frames, rows), jnp.float32)
    for d in range(sources):
        keep = jnp.exp2((take(d, 0) - top) * scale)
        total = total + take(d, 1) * keep
        row = row + take(d, 2) * keep
        col = col + take(d, 3) * keep
    core = lax.rem(me, 2)
    lane = lax.broadcasted_iota(jnp.int32, (rows, tracks), 0) // heads
    where = lax.broadcasted_iota(jnp.int32, (rows, tracks), 1)
    lane = jnp.where(lane < tracks // 2, lane + core * (tracks // 2), lane - core * (tracks // 2))
    mean = (lane == where).astype(jnp.float32)
    for k, (v, size) in enumerate(((row, GH), (col, GW))):
        coarse_ref[k] = lax.dot_general(
            v / total,
            mean,
            (((1,), (0,)), ((), ())),
            precision=lax.Precision.HIGHEST,
            preferred_element_type=jnp.float32,
        ) * (4.0 / (heads * size))
    for k in range(2):
        fine = ins[0][k]
        for j in range(1, pieces):
            fine = fine + ins[j][k]
        fine_ref[k] = fine


def finish(stats, pieces, heads, channels):
    quarter = stats.shape[2]
    rows = stats.shape[1] * 128
    return pl.pallas_call(
        functools.partial(finish_kernel, len(pieces), heads, channels),
        out_shape=[
            jax.ShapeDtypeStruct((2, quarter // 4, rows // heads), jnp.float32),
            jax.ShapeDtypeStruct(pieces[0].shape, jnp.float32),
        ],
        in_specs=[VMEM] * (1 + len(pieces)),
        out_specs=[VMEM, VMEM],
        compiler_params=SMALL,
        name="finish",
    )(stats, *pieces)


def body(coarse_query, coarse_feat, fine_query, fine_tiles, track_pos, tile_list, tile_valid):
    tracks, heads, channels = coarse_query.shape
    blocks = lax.axis_size("blk")
    owners = lax.axis_size("frames")
    region = coarse_feat.shape[1]
    window = track_pos.shape[1]
    own = fine_query.shape[0]

    def swap(x, j):
        return lax.ppermute(x, "frames", [(i, i ^ j) for i in range(owners)])

    ranks = [sorted(range(blocks), key=lambda b: (abs(b - blocks // 2), b))]
    halves = coarse_query.reshape(2, tracks * heads // 2, channels)
    mine, payload = prepare(blocks, halves, fine_query, jnp.transpose(track_pos, (0, 2, 1)))
    first = lax.all_to_all(
        mine, "blk", split_axis=0, concat_axis=0, tiled=True, axis_index_groups=ranks
    )
    payloads = [payload] + [swap(payload, j) for j in range(1, owners)]
    tiles, codes = fetch(tile_list, tile_valid, fine_tiles, owners, own)
    fine = fine_part(codes, tiles, own, window, region, payloads)
    gate = fine[0]
    fine = [fine[0]] + [swap(fine[j], j) for j in range(1, owners)]

    cells = jnp.transpose(coarse_feat, (1, 0, 2))
    second = swap(first, 1)
    stats = coarse_half(first, cells, gate)
    stats = coarse_half(second, cells, gate, stats)
    stats = lax.all_to_all(
        stats, "blk", split_axis=0, concat_axis=0, tiled=True, axis_index_groups=ranks
    )
    coarse_pos, fine_offset = finish(stats, fine, heads, channels)
    return coarse_pos, jnp.transpose(fine_offset, (0, 2, 1))


def solution(mesh):
    return jax.shard_map(
        body,
        mesh=mesh,
        in_specs=(
            P("blk", None, None),
            P("frames", "blk", None),
            P(("blk", "frames"), None),
            P("frames", "blk", None, None),
            P(None, None, ("blk", "frames")),
            P("frames", "blk", None, None),
            P("frames", "blk", None, None),
        ),
        out_specs=(P(None, "frames", "blk"), P(None, None, ("blk", "frames"))),
        check_vma=False,
    )
```

```python
import functools
import math

import jax
import jax.numpy as jnp
from jax import lax
from jax.experimental import pallas as pl
from jax.experimental.pallas import tpu as pltpu
from jax.sharding import PartitionSpec as P


GH = 68
GW = 120
TILE = 8
LOW = -3e38
spread_cells = 32.0


VMEM = pl.BlockSpec(memory_space=pltpu.VMEM)
SMEM = pl.BlockSpec(memory_space=pltpu.SMEM)
ANY = pl.BlockSpec(memory_space=pl.ANY)
HBM = pl.BlockSpec(memory_space=pltpu.HBM)
SMALL = pltpu.CompilerParams(vmem_limit_bytes=8 << 20)
LARGE = pltpu.CompilerParams(vmem_limit_bytes=16 << 20)


def stay(x):
    return pltpu.with_memory_space_constraint(x, pltpu.HBM)


def prepare_kernel(
    pieces, own, halves_ref, query_ref, pos_ref, list_ref, valid_ref,
    mine_ref, pack_ref, ids_ref, codes_ref, half, query, pos, live, sems,
):
    blocks = mine_ref.shape[0]
    frames = ids_ref.shape[0]
    me = lax.axis_index("frames")
    reads = [
        pltpu.make_async_copy(src, dst, sems.at[k])
        for k, (src, dst) in enumerate(
            (
                (halves_ref.at[lax.rem(me, 2)], half),
                (query_ref, query),
                (pos_ref, pos),
                (list_ref, ids_ref),
                (valid_ref, live),
            )
        )
    ]
    writes = [pltpu.make_async_copy(half, mine_ref.at[k], sems.at[5 + k]) for k in range(blocks)]
    for copy in reads:
        copy.start()
    reads[0].wait()
    for copy in writes:
        copy.start()
    for copy in reads[1:]:
        copy.wait()
    window = pos.shape[2]
    pack_ref[...] = jnp.zeros(pack_ref.shape, jnp.float32)
    pack_ref[0:own, :] = query[...].astype(jnp.float32)
    for k in range(2):
        pack_ref[(k + 1) * own : (k + 2) * own, 0:window] = pos[k].astype(jnp.float32)
    for i in range(frames):
        for j in range(pieces):
            owner = pl.ds(lax.bitwise_xor(me, j), 1)
            code = jnp.where(live[i, 0, owner, :] > 0, ids_ref[i, 0, owner, :], -1)
            for k in range(own):
                row = (i * pieces + j) * own + k
                codes_ref[row : row + 1, :] = code.astype(jnp.float32)
    for copy in writes:
        copy.wait()


def prepare(blocks, pieces, halves, fine_query, places, tile_list, tile_valid):
    _, rows, channels = halves.shape
    own = fine_query.shape[0]
    frames, _, _, slots = tile_list.shape
    arrays = (halves, fine_query, places, tile_list, tile_valid)
    return pl.pallas_call(
        functools.partial(prepare_kernel, pieces, own),
        out_shape=[
            jax.ShapeDtypeStruct((blocks, rows, channels), halves.dtype),
            jax.ShapeDtypeStruct((8, fine_query.shape[1]), jnp.float32),
            jax.ShapeDtypeStruct(tile_list.shape, tile_list.dtype),
            jax.ShapeDtypeStruct((frames * pieces * own, slots), jnp.float32),
        ],
        in_specs=[HBM] * 5,
        out_specs=[HBM, VMEM, VMEM, VMEM],
        scratch_shapes=[
            pltpu.VMEM((rows, channels), halves.dtype),
            pltpu.VMEM(fine_query.shape, fine_query.dtype),
            pltpu.VMEM(places.shape, places.dtype),
            pltpu.VMEM(tile_valid.shape, tile_valid.dtype),
            pltpu.SemaphoreType.DMA((5 + blocks,)),
        ],
        compiler_params=SMALL,
        name="prepare",
    )(*(stay(x) for x in arrays))


def fetch_kernel(pieces, ids_ref, tiles_ref, out_ref, sems):
    frames, _, slots = out_ref.shape[:3]
    me = lax.axis_index("frames")
    for i in range(frames):
        for owner in range(pieces):
            slot = out_ref.at[i, lax.bitwise_xor(me, owner)]
            for s in range(slots):
                pltpu.make_async_copy(
                    tiles_ref.at[i, ids_ref[i, 0, owner, s]], slot.at[s], sems.at[i]
                ).start()
    for i in range(frames):
        pltpu.make_async_copy(out_ref.at[i], out_ref.at[i], sems.at[i]).wait()


def fetch(ids, fine_tiles, pieces):
    frames, _, cells, channels = fine_tiles.shape
    slots = ids.shape[3]
    return pl.pallas_call(
        functools.partial(fetch_kernel, pieces),
        out_shape=jax.ShapeDtypeStruct(
            (frames, pieces, slots, cells, channels), fine_tiles.dtype
        ),
        in_specs=[SMEM, HBM],
        out_specs=VMEM,
        scratch_shapes=[pltpu.SemaphoreType.DMA((frames,))],
        compiler_params=SMALL,
        name="fetch",
    )(ids, stay(fine_tiles))


def fine_kernel(pieces, own, region, codes_ref, tiles_ref, *refs):
    ins, evens, odd_ref = refs[:pieces], refs[pieces:-1], refs[-1]
    frames, _, slots, cells, channels = tiles_ref.shape
    tracks = pieces * own
    wide = slots * cells
    base = lax.axis_index("blk") * region
    me = lax.axis_index("frames")
    window = odd_ref.shape[3]
    scale = 1.0 / math.sqrt(channels)
    query = jnp.concatenate([r[0:own, :] for r in ins], axis=0).astype(jnp.bfloat16)
    rows_in = jnp.concatenate([r[own : 2 * own, :] for r in ins], axis=0)
    cols_in = jnp.concatenate([r[2 * own : 3 * own, :] for r in ins], axis=0)
    lane_in = lax.broadcasted_iota(jnp.int32, (tracks, channels), 1)
    spread = (
        lax.broadcasted_iota(jnp.int32, (slots, wide), 0)
        == lax.broadcasted_iota(jnp.int32, (slots, wide), 1) // cells
    ).astype(jnp.bfloat16)
    inner = lax.broadcasted_iota(jnp.int32, (tracks, wide), 1) % cells
    inner_row = (inner // TILE).astype(jnp.float32)
    inner_col = (inner % TILE).astype(jnp.float32)
    piece = lax.broadcasted_iota(jnp.int32, (tracks, wide), 0) // own
    lane_out = lax.broadcasted_iota(jnp.int32, (tracks, window), 1)
    rows_out = jnp.zeros((tracks, window), jnp.float32)
    cols_out = jnp.zeros((tracks, window), jnp.float32)
    codes = lax.dot_general(
        codes_ref[...].astype(jnp.bfloat16),
        spread,
        (((1,), (0,)), ((), ())),
        preferred_element_type=jnp.float32,
    )
    for i in range(frames):
        scores = None
        for j in range(pieces):
            got = lax.dot_general(
                query,
                tiles_ref[i, j].reshape(wide, channels),
                (((1,), (1,)), ((), ())),
                preferred_element_type=jnp.float32,
            )
            scores = got if scores is None else jnp.where(piece == j, got, scores)
        code = codes[i * tracks : (i + 1) * tracks]
        cell = code + base.astype(jnp.float32)
        tile_row = jnp.floor((cell + 0.5) * (1.0 / GW))
        tile_col = cell - GW * tile_row
        here = lane_in == me * frames + i
        track_row = jnp.sum(jnp.where(here, rows_in, 0.0), axis=1, keepdims=True)
        track_col = jnp.sum(jnp.where(here, cols_in, 0.0), axis=1, keepdims=True)
        off_row = (tile_row * TILE + inner_row) - track_row
        off_col = (tile_col * TILE + inner_col) - track_col
        distance = off_row * off_row + off_col * off_col
        scores = scores * scale - distance * (0.5 / (spread_cells * spread_cells))
        scores = jnp.where(code < -0.5, -1e30, scores)
        highest = jnp.max(scores, axis=1, keepdims=True)
        weights = jnp.exp(scores - highest)
        norm = 1.0 / (jnp.sum(weights, axis=1, keepdims=True) * spread_cells)
        mean_row = jnp.sum(weights * off_row, axis=1, keepdims=True) * norm
        mean_col = jnp.sum(weights * off_col, axis=1, keepdims=True) * norm
        rows_out = jnp.where(lane_out == me * frames + i, mean_row, rows_out)
        cols_out = jnp.where(lane_out == me * frames + i, mean_col, cols_out)
    for j in range(pieces):
        for k, v in enumerate((rows_out, cols_out)):
            piece_out = v[j * own : (j + 1) * own]
            if j % 2:
                odd_ref[j // 2, k] = piece_out
            else:
                evens[j // 2][k] = piece_out


def fine_part(codes, tiles, own, window, region, payloads):
    pieces = len(payloads)
    return pl.pallas_call(
        functools.partial(fine_kernel, pieces, own, region),
        out_shape=[jax.ShapeDtypeStruct((2, own, window), jnp.float32)] * (pieces // 2)
        + [jax.ShapeDtypeStruct((pieces // 2, 2, own, window), jnp.float32)],
        in_specs=[VMEM, VMEM] + [VMEM] * pieces,
        out_specs=[VMEM] * (pieces // 2 + 1),
        compiler_params=SMALL,
        name="fine_part",
    )(codes, tiles, *payloads)


def coarse_kernel(half, q_ref, f_ref, gate_ref, *rest):
    if half:
        prev_ref, o_ref, s_ref = rest
    else:
        o_ref, s_ref = rest
    region, frames, channels = f_ref.shape
    groups, rows, _ = q_ref.shape
    per = 256 // rows
    quads = groups // per
    cells = 8 // frames
    run = 15
    seg = run * cells
    factor = math.log2(math.e) / math.sqrt(channels)
    base = lax.axis_index("blk") * region
    sub = lax.broadcasted_iota(jnp.int32, (8, 128), 0)
    inside = (sub // frames).astype(jnp.float32)
    width = min(rows, 128)

    def fold(x):
        y = x
        for k in range(1, cells):
            y = y + pltpu.roll(x, k * frames, 0)
        return y

    def score(quad, at, n):
        q = q_ref[pl.ds(quad * per, per)].reshape(256, channels)
        block = f_ref[pl.ds(at, n)].reshape(n * frames, channels)
        return lax.dot_general(
            block, q, (((1,), (1,)), ((), ())), preferred_element_type=jnp.float32
        )

    def gather(d, at, n, tops, sums):
        out = []
        for lt in range(2):
            total, ramp, row_sum, col_sum = sums[lt]
            for k in range(n // seg):
                acc = None
                for j in range(run):
                    i = k * run + j
                    x = d[8 * i : 8 * i + 8, lt * 128 : (lt + 1) * 128]
                    if tops is not None:
                        x = x - tops[lt]
                    p = jnp.exp2(x * factor)
                    acc = p if acc is None else acc + p
                    ramp = ramp + acc
                first = base + (at + k * seg)
                row = first // GW
                col = first - row * GW
                total = total + acc
                row_sum = row_sum + acc * (row.astype(jnp.float32) - (GH - 1) / 2.0)
                col_sum = col_sum + acc * (col.astype(jnp.float32) - (GW - 1) / 2.0)
            out.append((total, ramp, row_sum, col_sum))
        return out

    zero = jnp.zeros((8, 128), jnp.float32)

    def store(quad, lt, top, sums):
        total, ramp, row_sum, col_sum = sums
        col_sum = col_sum + (run * total - ramp) * float(cells) + total * inside
        total = fold(total)
        for k in range(128 // width):
            column = lt * 128 + k * width
            group = quad * per + column // rows
            lane = half * rows + column % rows
            for st, v in enumerate((top, total, fold(row_sum), fold(col_sum))):
                o_ref[
                    group, lane // 128, st * frames : (st + 1) * frames, lane % 128 : lane % 128 + width
                ] = v[0:frames, k * width : (k + 1) * width]
        return total

    if half:
        if rows < 128:
            o_ref[:, :, :, 0:rows] = prev_ref[:, :, :, 0:rows]
        else:
            o_ref[:, 0 : rows // 128] = prev_ref[:, 0 : rows // 128]

    def plain(quad, worst):
        sums = [(zero, zero, zero, zero)] * 2
        for at in range(0, region, 4 * run):
            n = min(4 * run, region - at)
            sums = gather(score(quad, at, n), at, n, None, sums)
        for lt in range(2):
            total = store(quad, lt, zero, sums[lt])
            good = (total >= 2.0**-90) & (total <= 2.0**100)
            worst = jnp.maximum(worst, jnp.where(good, 0.0, 1.0))
        return worst

    worst = lax.fori_loop(0, quads, plain, zero)

    @pl.when(jnp.max(worst) > 0.0)
    def _():
        chunks = region // seg

        def careful(quad, carry):
            def first(c, best):
                d = score(quad, c * seg, seg)
                s_ref[c] = d
                return jnp.maximum(best, jnp.max(d.reshape(run, 8, 256), axis=0))

            best = lax.fori_loop(0, chunks, first, jnp.full((8, 256), LOW, jnp.float32))
            tops = []
            for lt in range(2):
                top = best[:, lt * 128 : (lt + 1) * 128]
                full = top
                for k in range(1, cells):
                    full = jnp.maximum(full, pltpu.roll(top, k * frames, 0))
                tops.append(full)

            def second(c, sums):
                return gather(s_ref[c], c * seg, seg, tops, sums)

            sums = lax.fori_loop(0, chunks, second, [(zero, zero, zero, zero)] * 2)
            for lt in range(2):
                store(quad, lt, tops[lt], sums[lt])
            return carry

        lax.fori_loop(0, quads, careful, 0)


def coarse_half(q, f, gate, prev=None):
    region, frames, _ = f.shape
    groups, rows, _ = q.shape
    half = 0 if prev is None else 1
    seg = 15 * (8 // frames)
    return pl.pallas_call(
        functools.partial(coarse_kernel, half),
        out_shape=jax.ShapeDtypeStruct((groups, rows // 64, 4 * frames, 128), jnp.float32),
        in_specs=[VMEM, VMEM, ANY] + [VMEM] * half,
        out_specs=VMEM,
        scratch_shapes=[pltpu.VMEM((region // seg, seg * frames, 256), jnp.float32)],
        compiler_params=LARGE,
    )(q, f, gate, *([prev] if half else []))


def finish_kernel(pieces, heads, channels, stats_ref, met_ref, *refs):
    scale = math.log2(math.e) / math.sqrt(channels)
    ins, (coarse_ref, fine_ref) = refs[:pieces], refs[pieces:]
    me = lax.axis_index("frames")
    sources, tiles, quarter, _ = stats_ref.shape
    frames = quarter // 4
    rows = tiles * 128
    tracks = rows // heads

    def take(d, st):
        return jnp.concatenate(
            [stats_ref[d, t, st * frames : (st + 1) * frames, :] for t in range(tiles)], axis=1
        )

    top = take(0, 0)
    for d in range(1, sources):
        top = jnp.maximum(top, take(d, 0))
    total = jnp.zeros((frames, rows), jnp.float32)
    row = jnp.zeros((frames, rows), jnp.float32)
    col = jnp.zeros((frames, rows), jnp.float32)
    for d in range(sources):
        keep = jnp.exp2((take(d, 0) - top) * scale)
        total = total + take(d, 1) * keep
        row = row + take(d, 2) * keep
        col = col + take(d, 3) * keep
    core = lax.rem(me, 2)
    lane = lax.broadcasted_iota(jnp.int32, (rows, tracks), 0) // heads
    where = lax.broadcasted_iota(jnp.int32, (rows, tracks), 1)
    lane = jnp.where(lane < tracks // 2, lane + core * (tracks // 2), lane - core * (tracks // 2))
    mean = (lane == where).astype(jnp.float32)
    for k, (v, size) in enumerate(((row, GH), (col, GW))):
        coarse_ref[k] = lax.dot_general(
            v / total,
            mean,
            (((1,), (0,)), ((), ())),
            precision=lax.Precision.HIGHEST,
            preferred_element_type=jnp.float32,
        ) * (4.0 / (heads * size))
    for k in range(2):
        fine = met_ref[0, k]
        for piece in ins:
            fine = fine + piece[k]
        fine_ref[k] = fine


def finish(stats, met, pieces, heads, channels):
    quarter = stats.shape[2]
    rows = stats.shape[1] * 128
    return pl.pallas_call(
        functools.partial(finish_kernel, len(pieces), heads, channels),
        out_shape=[
            jax.ShapeDtypeStruct((2, quarter // 4, rows // heads), jnp.float32),
            jax.ShapeDtypeStruct(pieces[0].shape, jnp.float32),
        ],
        in_specs=[VMEM] * (2 + len(pieces)),
        out_specs=[VMEM, VMEM],
        compiler_params=SMALL,
        name="finish",
    )(stats, met, *pieces)


def body(coarse_query, coarse_feat, fine_query, fine_tiles, track_pos, tile_list, tile_valid):
    tracks, heads, channels = coarse_query.shape
    blocks = lax.axis_size("blk")
    owners = lax.axis_size("frames")
    region = coarse_feat.shape[1]
    window = track_pos.shape[1]
    own = fine_query.shape[0]

    def swap(x, j):
        return lax.ppermute(x, "frames", [(i, i ^ j) for i in range(owners)])

    ranks = [sorted(range(blocks), key=lambda b: (abs(b - blocks // 2), b))]
    halves = coarse_query.reshape(2, tracks * heads // 2, channels)
    mine, payload, ids, codes = prepare(
        blocks, owners, halves, fine_query, jnp.transpose(track_pos, (0, 2, 1)), tile_list, tile_valid
    )
    first = lax.all_to_all(
        mine, "blk", split_axis=0, concat_axis=0, tiled=True, axis_index_groups=ranks
    )
    payloads = [payload] + [swap(payload, j) for j in range(1, owners)]
    tiles = fetch(ids, fine_tiles, owners)
    fine = fine_part(codes, tiles, own, window, region, payloads)
    evens, odd = fine[:-1], fine[-1]
    gate = evens[0]
    met = swap(odd, 1)
    far = [swap(evens[e] + met[e], 2 * e) for e in range(1, owners // 2)]

    cells = jnp.transpose(coarse_feat, (1, 0, 2))
    second = swap(first, 1)
    stats = coarse_half(first, cells, gate)
    stats = coarse_half(second, cells, gate, stats)
    stats = lax.all_to_all(
        stats, "blk", split_axis=0, concat_axis=0, tiled=True, axis_index_groups=ranks
    )
    coarse_pos, fine_offset = finish(stats, met, [gate] + far, heads, channels)
    return coarse_pos, jnp.transpose(fine_offset, (0, 2, 1))


def solution(mesh):
    return jax.shard_map(
        body,
        mesh=mesh,
        in_specs=(
            P("blk", None, None),
            P("frames", "blk", None),
            P(("blk", "frames"), None),
            P("frames", "blk", None, None),
            P(None, None, ("blk", "frames")),
            P("frames", "blk", None, None),
            P("frames", "blk", None, None),
        ),
        out_specs=(P(None, "frames", "blk"), P(None, None, ("blk", "frames"))),
        check_vma=False,
    )
```
